32 devices in a mesh: seq: 8 (over z, x), dp: 4 (over y, core).
Axes of the slice: x: 2, y: 2, z: 4, core: 2. Of those that a mesh axis runs over, the one named last changes fastest.
Arguments:
- bases: int32 [4, 16384], P('dp', 'seq'), may hold values from 0 to 3
- stem_table: bfloat16 [60, 256], replicated, may hold values from -1.5 to 1.5
- first_conv_taps: bfloat16 [3, 256, 128], replicated, may hold values from -0.21875 to 0.21875
- first_projection_weight: bfloat16 [128, 256], replicated, may hold values from -0.5 to 0.5
- second_conv_taps: bfloat16 [3, 256, 128], replicated, may hold values from -0.21875 to 0.21875
- second_projection_weight: bfloat16 [128, 256], replicated, may hold values from -0.5 to 0.5
- bin_weight: bfloat16 [1536, 256], P('seq'), may hold values from -0.375 to 0.375
- cotangent: bfloat16 [4, 1536, 128], P('dp', 'seq'), may hold values from -96 to 96
Outputs:
- predictions: bfloat16 [4, 1536, 128], P('dp', 'seq')
- saliency: float32 [4, 4, 16384], P('dp', None, 'seq')
- conv_one_grad: float32 [3, 256, 128], replicated
- proj_one_grad: float32 [128, 256], replicated
- conv_two_grad: float32 [3, 256, 128], replicated
- proj_two_grad: float32 [128, 256], replicated
- bin_weight_grad: float32 [1536, 256], P('seq')
The draws below stay inside these ranges and needn't reach their ends.
All inputs are finite; a program needn't handle non-finite values.
Results may differ from the reference program's by a relative error of at most 0.015.
Values may be sent and summed in bfloat16 or wider, within the bound.
A program may use at most 64 MiB of HBM per device.

```python
import jax
import jax.numpy as jnp
from jax import lax

C = 256
HID = 128
C_BIN = 1536
STEM = 15
POOL = 128
FIRST_DILATION = 2048
SECOND_DILATION = 4096
LENGTH = 16384
BINS = 128
WINDOWS = 4


def place_ends(drawn, key, least, largest):
    longest = drawn.shape.index(max(drawn.shape))
    spots = []
    for shift in (0, 1):
        where = [jax.random.randint(jax.random.fold_in(key, axis), (), 0, length) for axis, length in enumerate(drawn.shape)]
        where[longest] = (where[longest] + shift) % drawn.shape[longest]
        spots.append(tuple(where))
    return drawn.at[spots[0]].set(least).at[spots[1]].set(largest)


def strengthened(values, key, source, target, shards_of, factor):
    owner, partner = [(jnp.arange(values.shape[dim]) // (values.shape[dim] // shards_of)).reshape([-1 if axis == dim else 1 for axis in range(values.ndim)]) for dim in (source, target)]
    chosen = jax.random.permutation(key, shards_of)[partner]
    strong = (owner == chosen) | (owner == (partner + shards_of // 2) % shards_of)
    return jnp.where(strong, factor * values, values)


def level_of(key, dims, cuts, low, largest):
    def one(position, shards_of):
        steps = jax.random.uniform(jax.random.fold_in(jax.random.fold_in(key, 6), position), (shards_of,), jnp.float32, low / len(cuts), largest / len(cuts))
        return jnp.repeat(jnp.exp(steps), dims[position] // shards_of).reshape((-1,) + (1,) * (len(dims) - position - 1))

    level = one(*cuts[0])
    for cut in cuts[1:]:
        level = level * one(*cut)
    return level


def bell_draw(key, shape, scale, most, shards=(), kind=jnp.bfloat16):
    entries = jax.random.normal(key, shape, jnp.float32) * scale
    if len(shards) > 0:
        entries = level_of(key, shape, shards, -0.22, 0.18) * entries
    return jnp.clip(entries, min=-most, max=most).astype(kind)


def bell_draw_with(own_key, extent, scale, most, shards, heavy, held_as=jnp.bfloat16):
    values = scale * jax.random.normal(own_key, extent, jnp.float32)
    if shards:
        values = values * level_of(own_key, extent, shards, -0.22, 0.18)
    return jnp.clip(strengthened(values, jax.random.fold_in(own_key, 3), *heavy), -most, most).astype(held_as)


def setup_inputs(seed: int = 0) -> dict:
    arg_keys = jax.random.split(jax.random.key(seed), 9)
    return {
        "bases": place_ends(jax.random.randint(arg_keys[0], (WINDOWS, LENGTH), 0, 4), jax.random.fold_in(arg_keys[0], 1), 0, 3).astype(jnp.int32),
        "stem_table": bell_draw(arg_keys[1], (4 * STEM, C), STEM ** -0.5, 1.5),
        "first_conv_taps": bell_draw(arg_keys[2], (3, C, HID), (3 * C) ** -0.5, 0.21875),
        "first_projection_weight": bell_draw(arg_keys[3], (HID, C), HID ** -0.5, 0.5),
        "second_conv_taps": bell_draw(arg_keys[4], (3, C, HID), (3 * C) ** -0.5, 0.21875),
        "second_projection_weight": bell_draw(arg_keys[5], (HID, C), HID ** -0.5, 0.5),
        "bin_weight": bell_draw(arg_keys[6], (C_BIN, C), C ** -0.5, 0.375, ((0, 8),)),
        "cotangent": bell_draw_with(arg_keys[7], (WINDOWS, C_BIN, BINS), 16.0, 96.0, ((0, 4), (1, 8)), (1, 2, 8, 2.0)),
    }


def gelu_exact(value):
    return 0.5 * value * (1.0 + jax.scipy.special.erf(value * 0.7071067811865476))


def gelu_slope(value):
    return 0.5 * (1.0 + jax.scipy.special.erf(value * 0.7071067811865476)) + value * jnp.exp(-0.5 * value * value) * 0.3989422804014327


def shift_rows(values, offset):
    zeros = jnp.zeros((abs(offset),) + values.shape[1:], values.dtype)
    if offset > 0:
        return jnp.concatenate([zeros, values[:-offset]], axis=0)
    return jnp.concatenate([values[-offset:], zeros], axis=0)


def stem_codes(bases_row):
    count = bases_row.shape[0]
    half = STEM // 2
    padded = jnp.pad((bases_row + 1).astype(jnp.int32), half)
    taps = jnp.stack([padded[k:k + count] for k in range(STEM)], axis=1)
    letters = jnp.arange(1, 5, dtype=jnp.int32)
    return (taps[:, :, None] == letters[None, None, :]).astype(jnp.bfloat16).reshape(count, 4 * STEM)


def residual_block_apply(stream, conv_w, proj_w, reach):
    act = gelu_exact(stream.astype(jnp.float32)).astype(jnp.bfloat16)
    before = shift_rows(act, reach)
    after = shift_rows(act, -reach)
    tap_before = jnp.dot(before, conv_w[0], preferred_element_type=jnp.float32).astype(jnp.bfloat16)
    tap_after = jnp.dot(after, conv_w[2], preferred_element_type=jnp.float32).astype(jnp.bfloat16)
    pre = jnp.dot(act, conv_w[1], preferred_element_type=jnp.float32)
    pre = pre + tap_before.astype(jnp.float32) + tap_after.astype(jnp.float32)
    inner = gelu_exact(pre).astype(jnp.bfloat16)
    result = (stream.astype(jnp.float32) + jnp.dot(inner, proj_w, preferred_element_type=jnp.float32)).astype(jnp.bfloat16)
    return result, (stream, act, before, after, pre, inner)


def residual_block_reverse(incoming, saved, conv_w, proj_w, reach):
    stream, act, before, after, pre, inner = saved
    grad_in = incoming.astype(jnp.bfloat16)
    proj_raw = jnp.dot(inner.T, grad_in, preferred_element_type=jnp.float32)
    inner_grad = jnp.dot(grad_in, proj_w.T, preferred_element_type=jnp.float32)
    pre_grad = (inner_grad * gelu_slope(pre)).astype(jnp.bfloat16)
    conv_raw = jnp.stack([jnp.dot(before.T, pre_grad, preferred_element_type=jnp.float32),
                          jnp.dot(act.T, pre_grad, preferred_element_type=jnp.float32),
                          jnp.dot(after.T, pre_grad, preferred_element_type=jnp.float32)])
    act_grad = jnp.dot(pre_grad, conv_w[1].T, preferred_element_type=jnp.float32)
    act_grad = act_grad + jnp.dot(shift_rows(pre_grad, -reach), conv_w[0].T, preferred_element_type=jnp.float32)
    act_grad = act_grad + jnp.dot(shift_rows(pre_grad, reach), conv_w[2].T, preferred_element_type=jnp.float32)
    outgoing = incoming + act_grad * gelu_slope(stream.astype(jnp.float32))
    return outgoing, conv_raw, proj_raw


def one_window(bases_row, cot_window, stem_table, first_conv_taps, first_projection_weight, second_conv_taps, second_projection_weight, bin_weight):
    count = bases_row.shape[0]
    half = STEM // 2
    codes = stem_codes(bases_row)
    stem_pre = jnp.dot(codes, stem_table, preferred_element_type=jnp.float32)
    residual_input_level = gelu_exact(stem_pre).astype(jnp.bfloat16)
    residual_after_first, first_block_stash = residual_block_apply(residual_input_level, first_conv_taps, first_projection_weight, FIRST_DILATION)
    residual_after_second, second_block_stash = residual_block_apply(residual_after_first, second_conv_taps, second_projection_weight, SECOND_DILATION)
    pooled = jnp.mean(residual_after_second.astype(jnp.float32).reshape(count // POOL, POOL, residual_after_second.shape[1]), axis=1)
    pooled_act = gelu_exact(pooled).astype(jnp.bfloat16)
    preds = jnp.dot(bin_weight, pooled_act.T, preferred_element_type=jnp.float32).astype(jnp.bfloat16)
    bin_raw = jnp.dot(cot_window, pooled_act, preferred_element_type=jnp.float32)
    pooled_grad = jnp.dot(cot_window.T, bin_weight, preferred_element_type=jnp.float32) * gelu_slope(pooled)
    gradient_after_second = jnp.repeat(pooled_grad / POOL, POOL, axis=0)
    gradient_after_first, second_conv_init, second_projection_init = residual_block_reverse(gradient_after_second, second_block_stash, second_conv_taps, second_projection_weight, SECOND_DILATION)
    gradient_input_level, first_conv_init, first_projection_init = residual_block_reverse(gradient_after_first, first_block_stash, first_conv_taps, first_projection_weight, FIRST_DILATION)
    stem_grad = (gradient_input_level * gelu_slope(stem_pre)).astype(jnp.bfloat16)
    code_grad = jnp.dot(stem_grad, stem_table.T, preferred_element_type=jnp.float32)
    padded = jnp.pad(code_grad, ((half, half), (0, 0)))
    total = jnp.zeros((count, 4), jnp.float32)
    for k in range(STEM):
        start = 2 * half - k
        total = total + padded[start:start + count, 4 * k:4 * k + 4]
    return preds, total.T, first_conv_init, first_projection_init, second_conv_init, second_projection_init, bin_raw


def reference(bases, stem_table, first_conv_taps, first_projection_weight, second_conv_taps, second_projection_weight, bin_weight, cotangent):
    def per_window(pair):
        return one_window(pair[0], pair[1], stem_table, first_conv_taps, first_projection_weight, second_conv_taps, second_projection_weight, bin_weight)

    preds, saliency, first_conv_init, first_projection_init, second_conv_init, second_projection_init, bin_raw = lax.map(per_window, (bases, cotangent))
    scale = float(WINDOWS * LENGTH) ** -0.5
    return (preds, saliency,
            jnp.sum(first_conv_init, axis=0) * scale, jnp.sum(first_projection_init, axis=0) * scale,
            jnp.sum(second_conv_init, axis=0) * scale, jnp.sum(second_projection_init, axis=0) * scale,
            jnp.sum(bin_raw, axis=0) * scale)
```

```python
import functools

import jax
import jax.numpy as jnp
from jax import lax
from jax.experimental import pallas as pl
from jax.experimental.pallas import tpu as pltpu
from jax.sharding import PartitionSpec as P

STEM = 15
POOL = 128


def passed_along(value, axis, steps):
    count = lax.axis_size(axis)
    first, last = (max(0, -steps), min(count, count - steps))
    return lax.ppermute(value, axis, [(source, source + steps) for source in range(first, last)])


def with_halo(cells, sides, width):
    for axis, dim in sides:
        count = lax.axis_size(axis)
        ends = count - 1
        head = lax.slice_in_dim(cells, 0, width, axis=dim)
        tail = lax.slice_in_dim(cells, cells.shape[dim] - width, cells.shape[dim], axis=dim)
        cells = jnp.concatenate(
            [
                lax.ppermute(tail, axis, [(i, (i + 1) % count) for i in range(ends)]),
                cells,
                lax.ppermute(head, axis, [((i + 1) % count, i) for i in range(ends)]),
            ],
            axis=dim,
        )
    return cells


def gelu_exact(value):
    return 0.5 * value * (1.0 + jax.scipy.special.erf(value * 0.7071067811865476))


def gelu_slope(value):
    return (
        0.5 * (1.0 + jax.scipy.special.erf(value * 0.7071067811865476))
        + value * jnp.exp(-0.5 * value * value) * 0.3989422804014327
    )


def tap_shift(values, hops):
    return passed_along(values, "seq", hops)


def grad_shift(values, hops):
    return passed_along(values, "seq", hops)


def reduce_grads(conv_raw, proj_raw):
    return lax.psum((conv_raw, proj_raw), ("seq", "dp"))


def residual_block_apply(stream, conv_w, proj_w, hops):
    act = gelu_exact(stream.astype(jnp.float32)).astype(jnp.bfloat16)
    before = tap_shift(act, hops)
    after = tap_shift(act, -hops)
    tap_before = jnp.dot(before, conv_w[0], preferred_element_type=jnp.float32).astype(jnp.bfloat16)
    tap_after = jnp.dot(after, conv_w[2], preferred_element_type=jnp.float32).astype(jnp.bfloat16)
    pre = jnp.dot(act, conv_w[1], preferred_element_type=jnp.float32)
    pre = pre + tap_before.astype(jnp.float32) + tap_after.astype(jnp.float32)
    inner = gelu_exact(pre).astype(jnp.bfloat16)
    result = (
        stream.astype(jnp.float32) + jnp.dot(inner, proj_w, preferred_element_type=jnp.float32)
    ).astype(jnp.bfloat16)
    return (result, (stream, act, before, after, pre, inner))


def residual_block_reverse(incoming, saved, conv_w, proj_w, hops):
    stream, act, before, after, pre, inner = saved
    grad_in = incoming.astype(jnp.bfloat16)
    inner_grad = jnp.dot(grad_in, proj_w.T, preferred_element_type=jnp.float32)
    pre_grad = (inner_grad * gelu_slope(pre)).astype(jnp.bfloat16)
    later = grad_shift(pre_grad, -hops)
    earlier = grad_shift(pre_grad, hops)
    proj_raw = jnp.dot(inner.T, grad_in, preferred_element_type=jnp.float32)
    middle = jnp.dot(act.T, pre_grad, preferred_element_type=jnp.float32)
    conv_raw = jnp.stack(
        [
            jnp.dot(before.T, pre_grad, preferred_element_type=jnp.float32),
            middle,
            jnp.dot(after.T, pre_grad, preferred_element_type=jnp.float32),
        ]
    )
    act_grad = jnp.dot(pre_grad, conv_w[1].T, preferred_element_type=jnp.float32)
    act_grad = act_grad + jnp.dot(later, conv_w[0].T, preferred_element_type=jnp.float32)
    act_grad = act_grad + jnp.dot(earlier, conv_w[2].T, preferred_element_type=jnp.float32)
    outgoing = incoming + act_grad * gelu_slope(stream.astype(jnp.float32))
    conv_sum, proj_sum = reduce_grads(conv_raw, proj_raw)
    return (outgoing, conv_sum, proj_sum)


def per_device(
    bases,
    stem_table,
    first_conv_taps,
    first_projection_weight,
    second_conv_taps,
    second_projection_weight,
    bin_weight,
    cotangent,
):
    length = bases.shape[1]
    width = stem_table.shape[1]
    half = STEM // 2
    bins_dev = length // POOL
    scale = float(lax.axis_size("dp") * lax.axis_size("seq") * length) ** (-0.5)
    padded_ids = with_halo(bases[0] + 1, (("seq", 0),), half)
    taps = jnp.stack([padded_ids[k : k + length] for k in range(STEM)], axis=1)
    letters = jnp.arange(1, 5, dtype=jnp.int32)
    codes = (
        (taps[:, :, None] == letters[None, None, :]).astype(jnp.bfloat16).reshape(length, 4 * STEM)
    )
    stem_pre = jnp.dot(codes, stem_table, preferred_element_type=jnp.float32)
    residual_input_level = gelu_exact(stem_pre).astype(jnp.bfloat16)
    residual_after_first, first_block_stash = residual_block_apply(
        residual_input_level, first_conv_taps, first_projection_weight, 1
    )
    residual_after_second, second_block_stash = residual_block_apply(
        residual_after_first, second_conv_taps, second_projection_weight, 2
    )
    pooled = jnp.mean(
        residual_after_second.astype(jnp.float32).reshape(bins_dev, POOL, width), axis=1
    )
    pooled_act = gelu_exact(pooled).astype(jnp.bfloat16)
    cot_rows = cotangent[0]
    gathered = lax.all_gather(pooled_act, "seq", axis=0, tiled=True)
    preds = lax.dot_general(
        bin_weight, gathered, (((1,), (1,)), ((), ())), preferred_element_type=jnp.float32
    ).astype(jnp.bfloat16)
    bin_part = jnp.dot(cot_rows, gathered, preferred_element_type=jnp.float32)
    summed = lax.psum_scatter(
        lax.dot_general(
            cot_rows, bin_weight, (((0,), (0,)), ((), ())), preferred_element_type=jnp.float32
        ),
        "seq",
        scatter_dimension=0,
        tiled=True,
    )
    bin_total = lax.psum(bin_part, "dp")
    pooled_grad = summed * gelu_slope(pooled)
    gradient_after_second = jnp.repeat(pooled_grad / POOL, POOL, axis=0)
    gradient_after_first, conv_two_sum, proj_two_sum = residual_block_reverse(
        gradient_after_second, second_block_stash, second_conv_taps, second_projection_weight, 2
    )
    gradient_input_level, conv_one_sum, proj_one_sum = residual_block_reverse(
        gradient_after_first, first_block_stash, first_conv_taps, first_projection_weight, 1
    )
    stem_grad = (gradient_input_level * gelu_slope(stem_pre)).astype(jnp.bfloat16)
    code_grad = jnp.dot(stem_grad, stem_table.T, preferred_element_type=jnp.float32)
    padded_grad = with_halo(code_grad.astype(jnp.bfloat16), (("seq", 0),), half).astype(
        code_grad.dtype
    )
    total = jnp.zeros((length, 4), jnp.float32)
    for k in range(STEM):
        start = 2 * half - k
        total = total + padded_grad[start : start + length, 4 * k : 4 * k + 4]
    return (
        preds[None],
        total.T[None],
        conv_one_sum * scale,
        proj_one_sum * scale,
        conv_two_sum * scale,
        proj_two_sum * scale,
        bin_total * scale,
    )


NN = (((1,), (0,)), ((), ()))
NT = (((1,), (1,)), ((), ()))
TN = (((0,), (0,)), ((), ()))
F32 = jnp.float32
BF16 = jnp.bfloat16
WIRE = jnp.bfloat16


def mm(left, right, dims=NN):
    return lax.dot_general(left, right, dims, preferred_element_type=F32)


def gelu_pair(value):
    cdf = 0.5 + 0.5 * lax.erf(value * 0.7071067811865476)
    slope = cdf + value * (jnp.exp(-0.5 * value * value) * 0.3989422804014327)
    return value * cdf, slope


def tower_kernel(
    n_seq,
    n_dp,
    scale,
    bases_ref,
    stem_ref,
    conv1_ref,
    proj1_ref,
    conv2_ref,
    proj2_ref,
    binw_ref,
    cot_ref,
    preds_ref,
    sal_ref,
    conv1_out,
    proj1_out,
    conv2_out,
    proj2_out,
    bin_out,
    ids,
    stem_pad,
    slope_stem,
    stream0,
    act0,
    slope0,
    slope_pre1,
    inner1,
    stream1,
    act1,
    slope1,
    slope_pre2,
    pooled,
    inner_sum,
    bin_grad,
    bin_inner,
    pg2,
    pg1,
    grad1,
    wcat,
    part_out,
    part_in,
    pool_all,
    bin_all,
    conv_acc,
    proj_acc,
    rs_out,
    rs_in,
    rs2_out,
    rs2_in,
    ag,
    ag_all,
    sal_out,
    sal_in,
    send_sem,
    recv_sem,
):
    seq = lax.axis_index("seq")
    dp = lax.axis_index("dp")
    length = bases_ref.shape[1]
    width = stem_ref.shape[1]
    hid = proj1_ref.shape[0]
    seg = length // n_seq
    per_seg = seg // POOL
    n_bins = n_seq * per_seg
    half = STEM // 2

    barrier = pltpu.get_barrier_semaphore()
    for i in range(1, n_seq):
        pl.semaphore_signal(
            barrier,
            inc=1,
            device_id=(lax.rem(seq + i, n_seq), dp),
            device_id_type=pl.DeviceIdType.MESH,
        )
    for i in range(1, n_dp):
        pl.semaphore_signal(
            barrier,
            inc=1,
            device_id=(seq, lax.rem(dp + i, n_dp)),
            device_id_type=pl.DeviceIdType.MESH,
        )
    used = [0]

    def send(axis, source, target):
        count = n_seq if axis == "seq" else n_dp
        copies = []
        for i in range(1, count):
            if axis == "seq":
                peer = lax.rem(seq + i, count)
                where = (peer, dp)
            else:
                peer = lax.rem(dp + i, count)
                where = (seq, peer)
            slot = used[0]
            used[0] += 1
            copy = pltpu.make_async_remote_copy(
                src_ref=source(peer),
                dst_ref=target(i),
                send_sem=send_sem.at[slot],
                recv_sem=recv_sem.at[slot],
                device_id=where,
                device_id_type=pl.DeviceIdType.MESH,
            )
            copy.start()
            copies.append(copy)
        return copies

    def finish(copies):
        for copy in copies:
            copy.wait()

    def rows_of(chunk):
        return pl.ds(pl.multiple_of(chunk * seg, seg), seg)

    outside = jnp.full((1, 1, length), -1, jnp.int32)
    ids[pl.ds(0, 1)] = outside
    ids[pl.ds(n_seq + 1, 1)] = outside
    ids[pl.ds(seq + 1, 1)] = bases_ref[...].reshape(1, 1, length)
    pl.semaphore_wait(barrier, n_seq - 1 + n_dp - 1)
    ids_copies = send("seq", lambda peer: ids.at[seq + 1], lambda i: ids.at[seq + 1])

    bins_total = n_bins * n_seq
    nat = lax.broadcasted_iota(jnp.int32, (bins_total, bins_total), 0)
    got = lax.broadcasted_iota(jnp.int32, (bins_total, bins_total), 1)
    h_bits = per_seg.bit_length() - 1
    s_bits = n_seq.bit_length() - 1
    chunk_of = nat >> (h_bits + s_bits)
    owner_of = (nat >> h_bits) & (n_seq - 1)
    place = (owner_of << (h_bits + s_bits)) | (chunk_of << h_bits) | (nat & (per_seg - 1))
    perm = (place == got).astype(F32).astype(BF16)

    cot = cot_ref[...].reshape(cot_ref.shape[1], cot_ref.shape[2])
    cot_perm = mm(cot, perm).astype(BF16)
    part_out[...] = mm(cot_perm, binw_ref[...], TN).reshape(n_seq, n_bins, width)
    part_copies = send("seq", lambda peer: part_out.at[peer], lambda i: part_in.at[i - 1])

    stem_pad[...] = jnp.concatenate(
        [stem_ref[...].astype(F32), jnp.zeros((64 - 4 * STEM, width), F32)], axis=0
    ).astype(BF16)
    wcat[0] = jnp.concatenate([conv1_ref[0], conv1_ref[1], conv1_ref[2]], axis=1)
    wcat[1] = jnp.concatenate([conv2_ref[0], conv2_ref[1], conv2_ref[2]], axis=1)
    act0[pl.ds(0, seg)] = jnp.zeros((seg, width), BF16)
    act0[pl.ds((n_seq + 1) * seg, seg)] = jnp.zeros((seg, width), BF16)
    act1[pl.ds(0, 2 * seg)] = jnp.zeros((2 * seg, width), BF16)
    act1[pl.ds((n_seq + 2) * seg, 2 * seg)] = jnp.zeros((2 * seg, width), BF16)
    pg1[pl.ds(0, seg)] = jnp.zeros((seg, hid), BF16)
    pg1[pl.ds((n_seq + 1) * seg, seg)] = jnp.zeros((seg, hid), BF16)
    pg2[pl.ds(0, 2 * seg)] = jnp.zeros((2 * seg, hid), BF16)
    pg2[pl.ds((n_seq + 2) * seg, 2 * seg)] = jnp.zeros((2 * seg, hid), BF16)
    sal_out[...] = jnp.zeros_like(sal_out)
    pooled[...] = jnp.zeros_like(pooled)
    inner_sum[...] = jnp.zeros_like(inner_sum)

    first = (seq == 0).astype(jnp.int32)
    last = (seq == n_seq - 1).astype(jnp.int32)
    low = pl.multiple_of(lax.rem(seq * seg + length - 128, length), 128)
    high = pl.multiple_of(lax.rem(seq * seg + seg, length), 128)
    span = seg + 256
    finish(ids_copies)

    def stem_chunk(chunk, carry):
        line = jnp.concatenate(
            [
                ids[chunk + 1 - first, :, pl.ds(low, 128)],
                ids[chunk + 1, :, pl.ds(pl.multiple_of(seq * seg, seg), seg)],
                ids[chunk + 1 + last, :, pl.ds(high, 128)],
            ],
            axis=1,
        )
        block = jnp.broadcast_to(line, (8, span))
        sub = lax.broadcasted_iota(jnp.int32, (8, span), 0)
        block = jnp.where(sub < 4, block, pltpu.roll(block, span - 1, 1))
        letter = (sub & 3)[:, :seg]
        tiles = []
        for m in range(8):
            moved = pltpu.roll(block, span - (128 - half + 2 * m), 1)[:, :seg]
            tiles.append((moved == letter).astype(F32))
        codes = jnp.concatenate(tiles, axis=0).astype(BF16)
        pre = mm(codes, stem_pad[...], TN)
        value, slope = gelu_pair(pre)
        rows = rows_of(chunk)
        slope_stem[rows] = slope
        value = value.astype(BF16)
        stream0[rows] = value
        act, slope = gelu_pair(value.astype(F32))
        slope0[rows] = slope
        act0[rows_of(chunk + 1)] = act.astype(BF16)
        return carry

    lax.fori_loop(0, n_seq, stem_chunk, 0)

    def pre_of(act, conv_ref, chunk, hops):
        wide = jnp.concatenate(
            [act[rows_of(chunk)], act[rows_of(chunk + hops)], act[rows_of(chunk + 2 * hops)]],
            axis=1,
        )
        return mm(wide, conv_ref[...].reshape(3 * width, hid))

    def first_chunk(chunk, carry):
        rows = rows_of(chunk)
        inner, slope = gelu_pair(pre_of(act0, conv1_ref, chunk, 1))
        slope_pre1[rows] = slope
        inner = inner.astype(BF16)
        inner1[rows] = inner
        result = (stream0[rows].astype(F32) + mm(inner, proj1_ref[...])).astype(BF16)
        stream1[rows] = result
        act, slope = gelu_pair(result.astype(F32))
        slope1[rows] = slope
        act1[rows_of(chunk + 2)] = act.astype(BF16)
        return carry

    lax.fori_loop(0, n_seq, first_chunk, 0)

    def second_chunk(chunk, carry):
        rows = rows_of(chunk)
        inner, slope = gelu_pair(pre_of(act1, conv2_ref, chunk, 2))
        slope_pre2[rows] = slope
        inner = inner.astype(BF16)
        result = (stream1[rows].astype(F32) + mm(inner, proj2_ref[...])).astype(BF16)
        bin_row = lax.broadcasted_iota(jnp.int32, (n_bins, seg), 0)
        bin_pos = lax.broadcasted_iota(jnp.int32, (n_bins, seg), 1) // POOL
        member = (bin_row == bin_pos + chunk * per_seg).astype(F32).astype(BF16)
        pooled[...] += mm(member, result)
        inner_sum[...] += mm(member, inner)
        return carry

    lax.fori_loop(0, n_seq, second_chunk, 0)

    pooled_act, pooled_slope = gelu_pair(pooled[...] * (1.0 / POOL))
    pool_all[pl.ds(seq, 1)] = pooled_act.astype(BF16).reshape(1, n_bins, width)
    pool_copies = send("seq", lambda peer: pool_all.at[seq], lambda i: pool_all.at[seq])

    finish(part_copies)
    total = part_out[seq]
    for i in range(n_seq - 1):
        total = total + part_in[i]
    grad2 = total * pooled_slope * (1.0 / POOL)
    bin_grad[...] = grad2
    grad2_in = grad2.astype(BF16)
    bin_inner[...] = mm(grad2_in, proj2_ref[...], NT)

    isum = inner_sum[...]
    coarse = isum.astype(BF16)
    fine = (isum - coarse.astype(F32)).astype(BF16)
    proj_acc[...] = mm(coarse, grad2_in, TN) + mm(fine, grad2_in, TN)

    def spread(ref, chunk, columns):
        return jnp.concatenate(
            [
                jnp.broadcast_to(ref[pl.ds(chunk * per_seg + h, 1), :], (POOL, columns))
                for h in range(per_seg)
            ],
            axis=0,
        )

    def grad2_chunk(chunk, carry):
        wide = spread(bin_inner, chunk, hid)
        pg2[rows_of(chunk + 2)] = (wide * slope_pre2[rows_of(chunk)]).astype(BF16)
        return carry

    lax.fori_loop(0, n_seq, grad2_chunk, 0)

    def around(pg, chunk, hops):
        return jnp.concatenate(
            [pg[rows_of(chunk + 2 * hops)], pg[rows_of(chunk + hops)], pg[rows_of(chunk)]], axis=1
        )

    def conv_grads(act, pg, hops):
        conv_acc[...] = jnp.zeros_like(conv_acc)

        def step(chunk, carry):
            conv_acc[...] += mm(act[rows_of(chunk + hops)], around(pg, chunk, hops), TN)
            return carry

        lax.fori_loop(0, n_seq, step, 0)

    piece = width // n_seq

    def reduce_one(b):
        for t in range(3):
            rs_out[b, t] = conv_acc[:, t * hid : (t + 1) * hid].astype(WIRE)
        for t in range(width // hid):
            rs_out[b, 3, pl.ds(t * hid, hid)] = proj_acc[:, t * hid : (t + 1) * hid].astype(WIRE)
        return send("dp", lambda peer: rs_out.at[b, peer], lambda i: rs_in.at[b, i - 1])

    def reduce_two(b, copies):
        finish(copies)
        total = rs_out[b, dp].astype(F32)
        for i in range(n_dp - 1):
            total = total + rs_in[b, i].astype(F32)
        rs2_out[b] = total.reshape(n_seq, piece, hid)
        return send("seq", lambda peer: rs2_out.at[b, peer], lambda i: rs2_in.at[b, i - 1])

    def reduce_three(b, copies):
        finish(copies)
        total = rs2_out[b, seq]
        for i in range(n_seq - 1):
            total = total + rs2_in[b, i]
        ag[b, pl.ds(seq, 1)] = (total * scale).astype(WIRE).reshape(1, piece, hid)
        return send("seq", lambda peer: ag.at[b, seq], lambda i: ag.at[b, seq])

    def reduce_four(b, copies):
        finish(copies)
        ag_all[b, pl.ds(dp, 1)] = ag[b].reshape(1, n_seq, piece, hid)
        return send("dp", lambda peer: ag.at[b], lambda i: ag_all.at[b, dp])

    def reduce_end(b, copies, conv_out, proj_out):
        finish(copies)
        for t in range(3):
            conv_out[t] = ag_all[b, t].reshape(width, hid).astype(F32)
        whole = ag_all[b, 3].reshape(width, hid).astype(F32)
        for t in range(width // hid):
            proj_out[:, t * hid : (t + 1) * hid] = whole[t * hid : (t + 1) * hid]

    conv_grads(act1, pg2, 2)
    two = reduce_one(0)

    finish(pool_copies)
    natural = mm(perm, pool_all[...].reshape(bins_total, width)).astype(BF16)
    preds_ref[...] = mm(binw_ref[...], natural, NT).astype(BF16).reshape(preds_ref.shape)
    bin_all[pl.ds(dp, 1)] = (
        mm(cot, natural).astype(WIRE).reshape(1, binw_ref.shape[0], width)
    )
    bin_copies = send("dp", lambda peer: bin_all.at[dp], lambda i: bin_all.at[dp])

    proj_acc[...] = jnp.zeros_like(proj_acc)

    def grad1_chunk(chunk, carry):
        rows = rows_of(chunk)
        act_grad = mm(around(pg2, chunk, 2), wcat[1], NT)
        grad = spread(bin_grad, chunk, width) + act_grad * slope1[rows]
        grad1[rows] = grad
        grad_in = grad.astype(BF16)
        pg1[rows_of(chunk + 1)] = (mm(grad_in, proj1_ref[...], NT) * slope_pre1[rows]).astype(BF16)
        proj_acc[...] += mm(inner1[rows], grad_in, TN)
        return carry

    lax.fori_loop(0, n_seq, grad1_chunk, 0)
    two = reduce_two(0, two)
    conv_grads(act0, pg1, 1)
    one = reduce_one(1)
    two = reduce_three(0, two)

    wide_out = seg + 128

    def saliency_chunk(chunk, carry):
        rows = rows_of(chunk)
        act_grad = mm(around(pg1, chunk, 1), wcat[0], NT)
        grad = grad1[rows] + act_grad * slope0[rows]
        stem_grad = (grad * slope_stem[rows]).astype(BF16)
        code_grad = mm(stem_pad[...], stem_grad, NT)
        code_grad = jnp.concatenate([code_grad, jnp.zeros((64, 128), F32)], axis=1)
        total = jnp.zeros((8, wide_out), F32)
        for m in range(8):
            shift = (2 * m - half) % wide_out
            tile = code_grad[8 * m : 8 * m + 8]
            total = total + (pltpu.roll(tile, shift, 1) if shift else tile)
        total = total[:4] + pltpu.roll(total, 1, 1)[4:]
        sal_out[chunk + 1, pl.ds(0, 4)] = total
        sal_out[chunk + 1 + jnp.where(seq == 0, -1, 1), pl.ds(4, 4)] = total
        return carry

    middle = n_seq // 2
    lax.fori_loop(0, middle, saliency_chunk, 0)
    one = reduce_two(1, one)
    two = reduce_four(0, two)
    lax.fori_loop(middle, n_seq, saliency_chunk, 0)
    sal_in[pl.ds(seq, 1)] = sal_out[pl.ds(seq + 1, 1)]
    sal_copies = send("seq", lambda peer: sal_out.at[peer + 1], lambda i: sal_in.at[seq])
    one = reduce_three(1, one)

    finish(bin_copies)
    total = bin_all[0].astype(F32)
    for d in range(1, n_dp):
        total = total + bin_all[d].astype(F32)
    bin_out[...] = total * scale
    reduce_end(0, two, conv2_out, proj2_out)
    one = reduce_four(1, one)

    finish(sal_copies)
    lane = lax.broadcasted_iota(jnp.int32, (4, 128), 1)

    def rest(s, row):
        return sal_in[s, row : row + 4, seg:]

    for s in range(n_seq):
        before = rest(s - 1, 0) if s > 0 else rest(n_seq - 1, 4)
        after = rest(s + 1, 0) if s < n_seq - 1 else rest(0, 4)
        block = sal_in[s, 0:4, 0:seg]
        sal_ref[0, :, s * seg : s * seg + 128] = block[:, :128] + jnp.where(lane < 64, before, 0.0)
        if seg > 256:
            sal_ref[0, :, s * seg + 128 : (s + 1) * seg - 128] = block[:, 128 : seg - 128]
        sal_ref[0, :, (s + 1) * seg - 128 : (s + 1) * seg] = block[:, seg - 128 :] + jnp.where(
            lane >= 64, after, 0.0
        )
    reduce_end(1, one, conv1_out, proj1_out)


def per_device_fused(
    bases,
    stem_table,
    first_conv_taps,
    first_projection_weight,
    second_conv_taps,
    second_projection_weight,
    bin_weight,
    cotangent,
):
    n_seq, n_dp = lax.axis_size("seq"), lax.axis_size("dp")
    length = bases.shape[1]
    width = stem_table.shape[1]
    hid = first_projection_weight.shape[0]
    seg = length // n_seq
    n_bins = length // POOL
    chans = bin_weight.shape[0]
    scale = float(n_dp * n_seq * length) ** (-0.5)
    copies = 5 * (n_seq - 1) + (n_dp - 1) + 2 * (2 * (n_seq - 1) + 2 * (n_dp - 1))
    vmem = pl.BlockSpec(memory_space=pltpu.VMEM)
    sds = jax.ShapeDtypeStruct
    piece = width // n_seq
    return pl.pallas_call(
        functools.partial(tower_kernel, n_seq, n_dp, scale),
        out_shape=(
            sds((1, chans, cotangent.shape[2]), BF16),
            sds((1, 4, length), F32),
            sds((3, width, hid), F32),
            sds((hid, width), F32),
            sds((3, width, hid), F32),
            sds((hid, width), F32),
            sds((chans, width), F32),
        ),
        in_specs=[vmem] * 8,
        out_specs=(vmem,) * 7,
        scratch_shapes=[
            pltpu.VMEM((n_seq + 2, 1, length), jnp.int32),
            pltpu.VMEM((64, width), BF16),
            pltpu.VMEM((length, width), F32),
            pltpu.VMEM((length, width), BF16),
            pltpu.VMEM((length + 2 * seg, width), BF16),
            pltpu.VMEM((length, width), F32),
            pltpu.VMEM((length, hid), F32),
            pltpu.VMEM((length, hid), BF16),
            pltpu.VMEM((length, width), BF16),
            pltpu.VMEM((length + 4 * seg, width), BF16),
            pltpu.VMEM((length, width), F32),
            pltpu.VMEM((length, hid), F32),
            pltpu.VMEM((n_bins, width), F32),
            pltpu.VMEM((n_bins, hid), F32),
            pltpu.VMEM((n_bins, width), F32),
            pltpu.VMEM((n_bins, hid), F32),
            pltpu.VMEM((length + 4 * seg, hid), BF16),
            pltpu.VMEM((length + 2 * seg, hid), BF16),
            pltpu.VMEM((length, width), F32),
            pltpu.VMEM((2, width, 3 * hid), BF16),
            pltpu.VMEM((n_seq, n_bins, width), F32),
            pltpu.VMEM((n_seq - 1, n_bins, width), F32),
            pltpu.VMEM((n_seq, n_bins, width), BF16),
            pltpu.VMEM((n_dp, chans, width), WIRE),
            pltpu.VMEM((width, 3 * hid), F32),
            pltpu.VMEM((hid, width), F32),
            pltpu.VMEM((2, n_dp, width, hid), WIRE),
            pltpu.VMEM((2, n_dp - 1, width, hid), WIRE),
            pltpu.VMEM((2, n_seq, piece, hid), F32),
            pltpu.VMEM((2, n_seq - 1, piece, hid), F32),
            pltpu.VMEM((2, n_seq, piece, hid), WIRE),
            pltpu.VMEM((2, n_dp, n_seq, piece, hid), WIRE),
            pltpu.VMEM((n_seq + 2, 8, seg + 128), F32),
            pltpu.VMEM((n_seq, 8, seg + 128), F32),
            pltpu.SemaphoreType.DMA((copies,)),
            pltpu.SemaphoreType.DMA((copies,)),
        ],
        compiler_params=pltpu.CompilerParams(
            collective_id=0, has_side_effects=True, vmem_limit_bytes=48 * 1024 * 1024
        ),
    )(
        bases,
        stem_table,
        first_conv_taps,
        first_projection_weight,
        second_conv_taps,
        second_projection_weight,
        bin_weight,
        cotangent,
    )


def fits_fused(mesh):
    n_seq, n_dp = mesh.shape["seq"], mesh.shape["dp"]
    return n_seq in (2, 4, 8) and n_dp == 4


def solution(mesh):
    placed = (P("dp", "seq"), P(), P(), P(), P(), P(), P("seq", None), P("dp", "seq", None))
    return jax.shard_map(
        per_device_fused if fits_fused(mesh) else per_device,
        mesh=mesh,
        in_specs=placed,
        out_specs=(P("dp", "seq", None), P("dp", None, "seq"), P(), P(), P(), P(), P("seq", None)),
        check_vma=False,
    )
```

```python
import functools

import jax
import jax.numpy as jnp
from jax import lax
from jax.experimental import pallas as pl
from jax.experimental.pallas import tpu as pltpu
from jax.sharding import PartitionSpec as P

STEM = 15
POOL = 128


def passed_along(value, axis, steps):
    count = lax.axis_size(axis)
    first, last = (max(0, -steps), min(count, count - steps))
    return lax.ppermute(value, axis, [(source, source + steps) for source in range(first, last)])


def with_halo(cells, sides, width):
    for axis, dim in sides:
        count = lax.axis_size(axis)
        ends = count - 1
        head = lax.slice_in_dim(cells, 0, width, axis=dim)
        tail = lax.slice_in_dim(cells, cells.shape[dim] - width, cells.shape[dim], axis=dim)
        cells = jnp.concatenate(
            [
                lax.ppermute(tail, axis, [(i, (i + 1) % count) for i in range(ends)]),
                cells,
                lax.ppermute(head, axis, [((i + 1) % count, i) for i in range(ends)]),
            ],
            axis=dim,
        )
    return cells


def gelu_exact(value):
    return 0.5 * value * (1.0 + jax.scipy.special.erf(value * 0.7071067811865476))


def gelu_slope(value):
    return (
        0.5 * (1.0 + jax.scipy.special.erf(value * 0.7071067811865476))
        + value * jnp.exp(-0.5 * value * value) * 0.3989422804014327
    )


def tap_shift(values, hops):
    return passed_along(values, "seq", hops)


def grad_shift(values, hops):
    return passed_along(values, "seq", hops)


def reduce_grads(conv_raw, proj_raw):
    return lax.psum((conv_raw, proj_raw), ("seq", "dp"))


def residual_block_apply(stream, conv_w, proj_w, hops):
    act = gelu_exact(stream.astype(jnp.float32)).astype(jnp.bfloat16)
    before = tap_shift(act, hops)
    after = tap_shift(act, -hops)
    tap_before = jnp.dot(before, conv_w[0], preferred_element_type=jnp.float32).astype(jnp.bfloat16)
    tap_after = jnp.dot(after, conv_w[2], preferred_element_type=jnp.float32).astype(jnp.bfloat16)
    pre = jnp.dot(act, conv_w[1], preferred_element_type=jnp.float32)
    pre = pre + tap_before.astype(jnp.float32) + tap_after.astype(jnp.float32)
    inner = gelu_exact(pre).astype(jnp.bfloat16)
    result = (
        stream.astype(jnp.float32) + jnp.dot(inner, proj_w, preferred_element_type=jnp.float32)
    ).astype(jnp.bfloat16)
    return (result, (stream, act, before, after, pre, inner))


def residual_block_reverse(incoming, saved, conv_w, proj_w, hops):
    stream, act, before, after, pre, inner = saved
    grad_in = incoming.astype(jnp.bfloat16)
    inner_grad = jnp.dot(grad_in, proj_w.T, preferred_element_type=jnp.float32)
    pre_grad = (inner_grad * gelu_slope(pre)).astype(jnp.bfloat16)
    later = grad_shift(pre_grad, -hops)
    earlier = grad_shift(pre_grad, hops)
    proj_raw = jnp.dot(inner.T, grad_in, preferred_element_type=jnp.float32)
    middle = jnp.dot(act.T, pre_grad, preferred_element_type=jnp.float32)
    conv_raw = jnp.stack(
        [
            jnp.dot(before.T, pre_grad, preferred_element_type=jnp.float32),
            middle,
            jnp.dot(after.T, pre_grad, preferred_element_type=jnp.float32),
        ]
    )
    act_grad = jnp.dot(pre_grad, conv_w[1].T, preferred_element_type=jnp.float32)
    act_grad = act_grad + jnp.dot(later, conv_w[0].T, preferred_element_type=jnp.float32)
    act_grad = act_grad + jnp.dot(earlier, conv_w[2].T, preferred_element_type=jnp.float32)
    outgoing = incoming + act_grad * gelu_slope(stream.astype(jnp.float32))
    conv_sum, proj_sum = reduce_grads(conv_raw, proj_raw)
    return (outgoing, conv_sum, proj_sum)


def per_device(
    bases,
    stem_table,
    first_conv_taps,
    first_projection_weight,
    second_conv_taps,
    second_projection_weight,
    bin_weight,
    cotangent,
):
    length = bases.shape[1]
    width = stem_table.shape[1]
    half = STEM // 2
    bins_dev = length // POOL
    scale = float(lax.axis_size("dp") * lax.axis_size("seq") * length) ** (-0.5)
    padded_ids = with_halo(bases[0] + 1, (("seq", 0),), half)
    taps = jnp.stack([padded_ids[k : k + length] for k in range(STEM)], axis=1)
    letters = jnp.arange(1, 5, dtype=jnp.int32)
    codes = (
        (taps[:, :, None] == letters[None, None, :]).astype(jnp.bfloat16).reshape(length, 4 * STEM)
    )
    stem_pre = jnp.dot(codes, stem_table, preferred_element_type=jnp.float32)
    residual_input_level = gelu_exact(stem_pre).astype(jnp.bfloat16)
    residual_after_first, first_block_stash = residual_block_apply(
        residual_input_level, first_conv_taps, first_projection_weight, 1
    )
    residual_after_second, second_block_stash = residual_block_apply(
        residual_after_first, second_conv_taps, second_projection_weight, 2
    )
    pooled = jnp.mean(
        residual_after_second.astype(jnp.float32).reshape(bins_dev, POOL, width), axis=1
    )
    pooled_act = gelu_exact(pooled).astype(jnp.bfloat16)
    cot_rows = cotangent[0]
    gathered = lax.all_gather(pooled_act, "seq", axis=0, tiled=True)
    preds = lax.dot_general(
        bin_weight, gathered, (((1,), (1,)), ((), ())), preferred_element_type=jnp.float32
    ).astype(jnp.bfloat16)
    bin_part = jnp.dot(cot_rows, gathered, preferred_element_type=jnp.float32)
    summed = lax.psum_scatter(
        lax.dot_general(
            cot_rows, bin_weight, (((0,), (0,)), ((), ())), preferred_element_type=jnp.float32
        ),
        "seq",
        scatter_dimension=0,
        tiled=True,
    )
    bin_total = lax.psum(bin_part, "dp")
    pooled_grad = summed * gelu_slope(pooled)
    gradient_after_second = jnp.repeat(pooled_grad / POOL, POOL, axis=0)
    gradient_after_first, conv_two_sum, proj_two_sum = residual_block_reverse(
        gradient_after_second, second_block_stash, second_conv_taps, second_projection_weight, 2
    )
    gradient_input_level, conv_one_sum, proj_one_sum = residual_block_reverse(
        gradient_after_first, first_block_stash, first_conv_taps, first_projection_weight, 1
    )
    stem_grad = (gradient_input_level * gelu_slope(stem_pre)).astype(jnp.bfloat16)
    code_grad = jnp.dot(stem_grad, stem_table.T, preferred_element_type=jnp.float32)
    padded_grad = with_halo(code_grad.astype(jnp.bfloat16), (("seq", 0),), half).astype(
        code_grad.dtype
    )
    total = jnp.zeros((length, 4), jnp.float32)
    for k in range(STEM):
        start = 2 * half - k
        total = total + padded_grad[start : start + length, 4 * k : 4 * k + 4]
    return (
        preds[None],
        total.T[None],
        conv_one_sum * scale,
        proj_one_sum * scale,
        conv_two_sum * scale,
        proj_two_sum * scale,
        bin_total * scale,
    )


NN = (((1,), (0,)), ((), ()))
NT = (((1,), (1,)), ((), ()))
TN = (((0,), (0,)), ((), ()))
F32 = jnp.float32
BF16 = jnp.bfloat16
WIRE = jnp.bfloat16
KERNEL_VMEM = 57 * 1024 * 1024


def mm(left, right, dims=NN):
    return lax.dot_general(left, right, dims, preferred_element_type=F32)


def gelu_pair(value):
    t = 1.0 / (1.0 + 0.23164188825 * jnp.abs(value))
    bell = jnp.exp2(value * value * -0.7213475204444817)
    tail = 0.5307027145 * t - 0.7265760135
    tail = tail * t + 0.7107068705
    tail = tail * t - 0.142248368
    tail = (tail * t + 0.127414796) * t * bell
    cdf = jnp.where(value >= 0.0, 1.0 - tail, tail)
    slope = cdf + value * (bell * 0.3989422804014327)
    return value * cdf, slope


def tower_kernel(
    n_seq,
    n_dp,
    scale,
    bases_in,
    stem_in,
    conv1_in,
    proj1_in,
    conv2_in,
    proj2_in,
    binw_in,
    cot_in,
    preds_out,
    sal_final,
    bin_final,
    ag_final,
    preds_ref,
    sal_ref,
    bin_out,
    store_sem,
    bases_ref,
    stem_ref,
    conv1_ref,
    proj1_ref,
    conv2_ref,
    proj2_ref,
    binw_ref,
    cot_ref,
    load_sem,
    stem_pad,
    slope_stem,
    stream0,
    act0,
    slope0,
    slope_pre1,
    inner1,
    stream1,
    act1,
    slope1,
    slope_pre2,
    pooled,
    inner_sum,
    bin_grad,
    bin_inner,
    pg2,
    pg1,
    grad1,
    wcat,
    part_out,
    part_in,
    pool_all,
    conv_acc,
    proj_acc,
    two_out,
    two_in,
    one_out,
    one_in,
    rs2_out,
    rs2_in,
    fin_out,
    fin_in,
    ag_all,
    sal_out,
    send_sem,
    recv_sem,
):
    seq = lax.axis_index("seq")
    dp = lax.axis_index("dp")
    loads = [
        pltpu.make_async_copy(source, target, load_sem.at[i])
        for i, (source, target) in enumerate(
            (
                (bases_in, bases_ref),
                (cot_in, cot_ref),
                (binw_in, binw_ref),
                (stem_in, stem_ref),
                (conv1_in, conv1_ref),
                (proj1_in, proj1_ref),
                (conv2_in, conv2_ref),
                (proj2_in, proj2_ref),
            )
        )
    ]
    for load in loads:
        load.start()
    length = bases_in.shape[1]
    width = stem_ref.shape[1]
    hid = proj1_ref.shape[0]
    seg = length // n_seq
    per_seg = seg // POOL
    n_bins = n_seq * per_seg
    half = STEM // 2

    barrier = pltpu.get_barrier_semaphore()
    for i in range(1, n_seq):
        pl.semaphore_signal(
            barrier,
            inc=1,
            device_id=(lax.rem(seq + i, n_seq), dp),
            device_id_type=pl.DeviceIdType.MESH,
        )
    for i in range(1, n_dp):
        pl.semaphore_signal(
            barrier,
            inc=1,
            device_id=(seq, lax.rem(dp + i, n_dp)),
            device_id_type=pl.DeviceIdType.MESH,
        )
    used = [0]

    def send(axis, source, target):
        count = n_seq if axis == "seq" else n_dp
        copies = []
        for i in range(1, count):
            if axis == "seq":
                peer = lax.rem(seq + i, count)
                where = (peer, dp)
            else:
                peer = lax.rem(dp + i, count)
                where = (seq, peer)
            slot = used[0]
            used[0] += 1
            copy = pltpu.make_async_remote_copy(
                src_ref=source(peer),
                dst_ref=target(i),
                send_sem=send_sem.at[slot],
                recv_sem=recv_sem.at[slot],
                device_id=where,
                device_id_type=pl.DeviceIdType.MESH,
            )
            copy.start()
            copies.append(copy)
        return copies

    def finish(copies):
        for copy in copies:
            copy.wait()

    def rows_of(chunk):
        return pl.ds(pl.multiple_of(chunk * seg, seg), seg)

    bins_total = n_bins * n_seq
    nat = lax.broadcasted_iota(jnp.int32, (bins_total, bins_total), 0)
    got = lax.broadcasted_iota(jnp.int32, (bins_total, bins_total), 1)
    h_bits = per_seg.bit_length() - 1
    s_bits = n_seq.bit_length() - 1
    chunk_of = nat >> (h_bits + s_bits)
    owner_of = (nat >> h_bits) & (n_seq - 1)
    place = (owner_of << (h_bits + s_bits)) | (chunk_of << h_bits) | (nat & (per_seg - 1))
    perm = (place == got).astype(F32).astype(BF16)

    for load in loads:
        load.wait()
    cot = cot_ref[...].reshape(cot_ref.shape[1], cot_ref.shape[2])
    cot_perm = mm(cot, perm).astype(BF16)
    part = mm(cot_perm, binw_ref[...], TN).reshape(n_seq, n_bins, width)
    ids = bases_ref[...].astype(F32)
    ids = jnp.concatenate([ids[:, i * seg : (i + 1) * seg] for i in range(n_seq)], axis=0)
    for i in range(n_seq):
        part_out[i, :n_bins] = part[i]
        part_out[i, n_bins:] = ids
    outside = jnp.full((1, n_seq, width), -1.0, F32)
    part_in[pl.ds(0, 1), n_bins:] = outside
    part_in[pl.ds(n_seq + 1, 1), n_bins:] = outside
    part_in[pl.ds(seq + 1, 1)] = part_out[pl.ds(seq, 1)]
    pl.semaphore_wait(barrier, n_seq - 1 + n_dp - 1)
    part_copies = send("seq", lambda peer: part_out.at[peer], lambda i: part_in.at[seq + 1])

    stem_pad[...] = jnp.concatenate(
        [stem_ref[...].astype(F32), jnp.zeros((64 - 4 * STEM, width), F32)], axis=0
    ).astype(BF16)
    wcat[0] = jnp.concatenate([conv1_ref[0], conv1_ref[1], conv1_ref[2]], axis=1)
    wcat[1] = jnp.concatenate([conv2_ref[0], conv2_ref[1], conv2_ref[2]], axis=1)
    act0[pl.ds(0, seg)] = jnp.zeros((seg, width), BF16)
    act0[pl.ds((n_seq + 1) * seg, seg)] = jnp.zeros((seg, width), BF16)
    act1[pl.ds(0, 2 * seg)] = jnp.zeros((2 * seg, width), BF16)
    act1[pl.ds((n_seq + 2) * seg, 2 * seg)] = jnp.zeros((2 * seg, width), BF16)
    pg1[pl.ds(0, seg)] = jnp.zeros((seg, hid), BF16)
    pg1[pl.ds((n_seq + 1) * seg, seg)] = jnp.zeros((seg, hid), BF16)
    pg2[pl.ds(0, 2 * seg)] = jnp.zeros((2 * seg, hid), BF16)
    pg2[pl.ds((n_seq + 2) * seg, 2 * seg)] = jnp.zeros((2 * seg, hid), BF16)
    sal_out[...] = jnp.zeros_like(sal_out)
    pooled[...] = jnp.zeros_like(pooled)
    inner_sum[...] = jnp.zeros_like(inner_sum)

    first = (seq == 0).astype(jnp.int32)
    last = (seq == n_seq - 1).astype(jnp.int32)
    row_before = lax.rem(seq + n_seq - 1, n_seq)
    row_after = lax.rem(seq + 1, n_seq)
    row_index = lax.broadcasted_iota(jnp.int32, (n_seq, seg), 0)

    def bases_row(slot, row):
        picked = jnp.where(row_index == row, part_in[slot, n_bins:], 0.0)
        return jnp.sum(picked, axis=0, keepdims=True)

    span = seg + 256
    finish(part_copies)

    def stem_chunk(chunk, carry):
        line = jnp.concatenate(
            [
                bases_row(chunk + 1 - first, row_before)[:, seg - 128 :],
                bases_row(chunk + 1, seq),
                bases_row(chunk + 1 + last, row_after)[:, :128],
            ],
            axis=1,
        )
        block = jnp.broadcast_to(line, (8, span))
        sub = lax.broadcasted_iota(jnp.int32, (8, span), 0)
        block = jnp.where(sub < 4, block, pltpu.roll(block, span - 1, 1))
        letter = (sub & 3)[:, :seg].astype(F32)
        tiles = []
        for m in range(8):
            moved = pltpu.roll(block, span - (128 - half + 2 * m), 1)[:, :seg]
            tiles.append((moved == letter).astype(F32))
        codes = jnp.concatenate(tiles, axis=0).astype(BF16)
        pre = mm(codes, stem_pad[...], TN)
        value, slope = gelu_pair(pre)
        rows = rows_of(chunk)
        slope_stem[rows] = slope
        value = value.astype(BF16)
        stream0[rows] = value
        act, slope = gelu_pair(value.astype(F32))
        slope0[rows] = slope
        act0[rows_of(chunk + 1)] = act.astype(BF16)
        return carry

    lax.fori_loop(0, n_seq, stem_chunk, 0)

    def pre_of(act, conv_ref, chunk, hops):
        wide = jnp.concatenate(
            [act[rows_of(chunk)], act[rows_of(chunk + hops)], act[rows_of(chunk + 2 * hops)]],
            axis=1,
        )
        return mm(wide, conv_ref[...].reshape(3 * width, hid))

    def first_chunk(chunk, carry):
        rows = rows_of(chunk)
        inner, slope = gelu_pair(pre_of(act0, conv1_ref, chunk, 1))
        slope_pre1[rows] = slope
        inner = inner.astype(BF16)
        inner1[rows] = inner
        result = (stream0[rows].astype(F32) + mm(inner, proj1_ref[...])).astype(BF16)
        stream1[rows] = result
        act, slope = gelu_pair(result.astype(F32))
        slope1[rows] = slope
        act1[rows_of(chunk + 2)] = act.astype(BF16)
        return carry

    lax.fori_loop(0, n_seq, first_chunk, 0)

    def second_chunk(chunk, carry):
        rows = rows_of(chunk)
        inner, slope = gelu_pair(pre_of(act1, conv2_ref, chunk, 2))
        slope_pre2[rows] = slope
        inner = inner.astype(BF16)
        result = (stream1[rows].astype(F32) + mm(inner, proj2_ref[...])).astype(BF16)
        bin_row = lax.broadcasted_iota(jnp.int32, (n_bins, seg), 0)
        bin_pos = lax.broadcasted_iota(jnp.int32, (n_bins, seg), 1) // POOL
        member = (bin_row == bin_pos + chunk * per_seg).astype(F32).astype(BF16)
        pooled[...] += mm(member, result)
        inner_sum[...] += mm(member, inner)
        return carry

    lax.fori_loop(0, n_seq, second_chunk, 0)

    pooled_act, pooled_slope = gelu_pair(pooled[...] * (1.0 / POOL))
    pool_all[pl.ds(seq, 1)] = pooled_act.astype(BF16).reshape(1, n_bins, width)
    pool_copies = send("seq", lambda peer: pool_all.at[seq], lambda i: pool_all.at[seq])

    total = part_in[1, :n_bins]
    for i in range(1, n_seq):
        total = total + part_in[i + 1, :n_bins]
    grad2 = total * pooled_slope * (1.0 / POOL)
    bin_grad[...] = grad2
    grad2_in = grad2.astype(BF16)
    bin_inner[...] = mm(grad2_in, proj2_ref[...], NT)

    isum = inner_sum[...]
    coarse = isum.astype(BF16)
    fine = (isum - coarse.astype(F32)).astype(BF16)
    proj_acc[...] = mm(coarse, grad2_in, TN) + mm(fine, grad2_in, TN)

    def spread(ref, chunk, columns):
        return jnp.concatenate(
            [
                jnp.broadcast_to(ref[pl.ds(chunk * per_seg + h, 1), :], (POOL, columns))
                for h in range(per_seg)
            ],
            axis=0,
        )

    def grad2_chunk(chunk, carry):
        wide = spread(bin_inner, chunk, hid)
        pg2[rows_of(chunk + 2)] = (wide * slope_pre2[rows_of(chunk)]).astype(BF16)
        return carry

    lax.fori_loop(0, n_seq, grad2_chunk, 0)

    def around(pg, chunk, hops):
        return jnp.concatenate(
            [pg[rows_of(chunk + 2 * hops)], pg[rows_of(chunk + hops)], pg[rows_of(chunk)]], axis=1
        )

    def conv_grads(act, pg, hops):
        conv_acc[...] = jnp.zeros_like(conv_acc)

        def step(chunk, carry):
            conv_acc[...] += mm(act[rows_of(chunk + hops)], around(pg, chunk, hops), TN)
            return carry

        lax.fori_loop(0, n_seq, step, 0)

    piece = width // n_seq
    n_chan = binw_ref.shape[0]

    def put_parts(target):
        for t in range(3):
            target[t, :width] = conv_acc[:, t * hid : (t + 1) * hid].astype(WIRE)
        for t in range(width // hid):
            target[3, t * hid : (t + 1) * hid] = proj_acc[:, t * hid : (t + 1) * hid].astype(WIRE)

    conv_grads(act1, pg2, 2)
    put_parts(two_out)
    two = send("dp", lambda peer: two_out.at[peer], lambda i: two_in.at[i - 1])

    finish(pool_copies)
    natural = mm(perm, pool_all[...].reshape(bins_total, width)).astype(BF16)
    preds_ref[...] = mm(binw_ref[...], natural, NT).astype(BF16).reshape(preds_ref.shape)
    bin_raw = mm(cot, natural).astype(WIRE)
    for d in range(n_dp):
        for t in range(width // hid):
            start = width + t * n_chan
            one_out[d, start : start + n_chan] = bin_raw[:, t * hid : (t + 1) * hid]
    stores = [
        pltpu.make_async_copy(preds_ref, preds_out, store_sem.at[0]),
        pltpu.make_async_copy(bin_out, bin_final, store_sem.at[1]),
        pltpu.make_async_copy(sal_ref, sal_final, store_sem.at[2]),
        pltpu.make_async_copy(ag_all, ag_final, store_sem.at[3]),
    ]
    stores[0].start()

    proj_acc[...] = jnp.zeros_like(proj_acc)

    def grad1_chunk(chunk, carry):
        rows = rows_of(chunk)
        act_grad = mm(around(pg2, chunk, 2), wcat[1], NT)
        grad = spread(bin_grad, chunk, width) + act_grad * slope1[rows]
        grad1[rows] = grad
        grad_in = grad.astype(BF16)
        pg1[rows_of(chunk + 1)] = (mm(grad_in, proj1_ref[...], NT) * slope_pre1[rows]).astype(BF16)
        proj_acc[...] += mm(inner1[rows], grad_in, TN)
        return carry

    lax.fori_loop(0, n_seq, grad1_chunk, 0)
    conv_grads(act0, pg1, 1)
    put_parts(one_out)
    one_in[pl.ds(dp, 1)] = one_out[pl.ds(dp, 1)]
    one = send("dp", lambda peer: one_out.at[peer], lambda i: one_in.at[dp])

    wide_out = seg + 128

    def saliency_chunk(chunk, carry):
        rows = rows_of(chunk)
        act_grad = mm(around(pg1, chunk, 1), wcat[0], NT)
        grad = grad1[rows] + act_grad * slope0[rows]
        stem_grad = (grad * slope_stem[rows]).astype(BF16)
        code_grad = mm(stem_pad[...], stem_grad, NT)
        code_grad = jnp.concatenate([code_grad, jnp.zeros((64, 128), F32)], axis=1)
        total = jnp.zeros((8, wide_out), F32)
        for m in range(8):
            shift = (2 * m - half) % wide_out
            tile = code_grad[8 * m : 8 * m + 8]
            total = total + (pltpu.roll(tile, shift, 1) if shift else tile)
        total = total[:4] + pltpu.roll(total, 1, 1)[4:]
        sal_out[chunk + 1, pl.ds(0, 4)] = total
        sal_out[chunk + 1 + jnp.where(seq == 0, -1, 1), pl.ds(4, 4)] = total
        return carry

    middle = n_seq // 2
    lax.fori_loop(0, middle, saliency_chunk, 0)
    finish(two)
    total = two_out[dp].astype(F32)
    for i in range(n_dp - 1):
        total = total + two_in[i].astype(F32)
    rs2_out[:, 0] = total.reshape(n_seq, piece, hid)
    finish(one)
    total = one_in[0, :width].astype(F32)
    for d in range(1, n_dp):
        total = total + one_in[d, :width].astype(F32)
    rs2_out[:, 1] = total.reshape(n_seq, piece, hid)
    summed = send("seq", lambda peer: rs2_out.at[peer], lambda i: rs2_in.at[i - 1])
    lax.fori_loop(middle, n_seq, saliency_chunk, 0)
    blank = jnp.zeros((8, 128), F32)
    for i in range(n_seq):
        cells = sal_out[i + 1]
        fin_out[i, 2 * piece :] = jnp.concatenate(
            [cells[:, :128], cells[:, 128:256], cells[:, 256:], blank], axis=0
        ).astype(WIRE)
    finish(summed)
    total = rs2_out[seq]
    for i in range(n_seq - 1):
        total = total + rs2_in[i]
    total = (total * scale).astype(WIRE).reshape(2 * piece, hid)
    for i in range(n_seq):
        fin_out[i, : 2 * piece] = total
    fin_in[pl.ds(seq, 1)] = fin_out[pl.ds(seq, 1)]
    last_copies = send("seq", lambda peer: fin_out.at[peer], lambda i: fin_in.at[seq])

    for t in range(width // hid):
        start = width + t * n_chan
        total = one_in[0, start : start + n_chan].astype(F32)
        for d in range(1, n_dp):
            total = total + one_in[d, start : start + n_chan].astype(F32)
        bin_out[:, t * hid : (t + 1) * hid] = total * scale
    stores[1].start()

    finish(last_copies)
    gathered = fin_in.at[:, pl.ds(0, 2 * piece)]
    ag_copies = send("dp", lambda peer: gathered, lambda i: ag_all.at[dp])
    ag_all[pl.ds(dp, 1)] = fin_in[:, : 2 * piece].reshape(1, n_seq, 2 * piece, hid)

    lane = lax.broadcasted_iota(jnp.int32, (4, 128), 1)

    spots = [fin_in[s, 2 * piece :].astype(F32) for s in range(n_seq)]

    def rest(s, row):
        return spots[s][16 + row : 20 + row]

    for s in range(n_seq):
        before = rest(s - 1, 0) if s > 0 else rest(n_seq - 1, 4)
        after = rest(s + 1, 0) if s < n_seq - 1 else rest(0, 4)
        sal_ref[0, :, s * seg : s * seg + 128] = spots[s][0:4] + jnp.where(lane < 64, before, 0.0)
        sal_ref[0, :, s * seg + 128 : (s + 1) * seg] = spots[s][8:12] + jnp.where(
            lane >= 64, after, 0.0
        )
    stores[2].start()
    finish(ag_copies)
    stores[3].start()
    for store in stores:
        store.wait()


def store_kernel(*refs):
    preds_in, sal_in, bin_in, ag_in = refs[:4]
    outs = refs[4:11]
    preds, sal, bins, ag, conv1, proj1, conv2, proj2, load_sem, store_sem = refs[11:]
    loads = [
        pltpu.make_async_copy(source, target, load_sem.at[i])
        for i, (source, target) in enumerate(
            ((ag_in, ag), (preds_in, preds), (sal_in, sal), (bin_in, bins))
        )
    ]
    for load in loads:
        load.start()
    stores = [
        pltpu.make_async_copy(source, target, store_sem.at[i])
        for i, (source, target) in enumerate(
            zip((preds, sal, conv1, proj1, conv2, proj2, bins), outs)
        )
    ]
    hid, width = proj1.shape
    piece = ag.shape[2] // 2
    loads[0].wait()
    for b, conv, proj, slot in ((0, conv2, proj2, 4), (1, conv1, proj1, 2)):
        for t in range(3):
            conv[t] = ag[t, :, b * piece : (b + 1) * piece].reshape(width, hid).astype(F32)
        stores[slot].start()
        whole = ag[3, :, b * piece : (b + 1) * piece].reshape(width, hid).astype(F32)
        for t in range(width // hid):
            proj[:, t * hid : (t + 1) * hid] = whole[t * hid : (t + 1) * hid]
        stores[slot + 1].start()
    for load, slot in zip(loads[1:], (0, 1, 6)):
        load.wait()
        stores[slot].start()
    for store in stores:
        store.wait()


def per_device_fused(
    bases,
    stem_table,
    first_conv_taps,
    first_projection_weight,
    second_conv_taps,
    second_projection_weight,
    bin_weight,
    cotangent,
):
    n_seq, n_dp = lax.axis_size("seq"), lax.axis_size("dp")
    length = bases.shape[1]
    width = stem_table.shape[1]
    hid = first_projection_weight.shape[0]
    seg = length // n_seq
    n_bins = length // POOL
    chans = bin_weight.shape[0]
    scale = float(n_dp * n_seq * length) ** (-0.5)
    copies = 4 * (n_seq - 1) + 3 * (n_dp - 1)
    rows = width + 2 * chans
    hbm = pl.BlockSpec(memory_space=pl.ANY)
    sds = jax.ShapeDtypeStruct
    piece = width // n_seq
    preds_shape = sds((1, chans, cotangent.shape[2]), BF16)
    sal_shape = sds((1, 4, length), F32)
    bin_shape = sds((chans, width), F32)
    conv_shape = sds((3, width, hid), F32)
    proj_shape = sds((hid, width), F32)
    room = lambda leaf: pltpu.VMEM(leaf.shape, leaf.dtype)
    made = pl.pallas_call(
        functools.partial(tower_kernel, n_seq, n_dp, scale),
        out_shape=(
            preds_shape,
            sal_shape,
            bin_shape,
            sds((n_dp, n_seq, 2 * piece, hid), WIRE),
        ),
        in_specs=[hbm] * 8,
        out_specs=(hbm,) * 4,
        scratch_shapes=[
            room(preds_shape),
            room(sal_shape),
            room(bin_shape),
            pltpu.SemaphoreType.DMA((4,)),
            pltpu.VMEM((1, length), jnp.int32),
            pltpu.VMEM(stem_table.shape, BF16),
            pltpu.VMEM(first_conv_taps.shape, BF16),
            pltpu.VMEM(first_projection_weight.shape, BF16),
            pltpu.VMEM(second_conv_taps.shape, BF16),
            pltpu.VMEM(second_projection_weight.shape, BF16),
            pltpu.VMEM(bin_weight.shape, BF16),
            pltpu.VMEM(cotangent.shape, BF16),
            pltpu.SemaphoreType.DMA((8,)),
            pltpu.VMEM((64, width), BF16),
            pltpu.VMEM((length, width), F32),
            pltpu.VMEM((length, width), BF16),
            pltpu.VMEM((length + 2 * seg, width), BF16),
            pltpu.VMEM((length, width), F32),
            pltpu.VMEM((length, hid), F32),
            pltpu.VMEM((length, hid), BF16),
            pltpu.VMEM((length, width), BF16),
            pltpu.VMEM((length + 4 * seg, width), BF16),
            pltpu.VMEM((length, width), F32),
            pltpu.VMEM((length, hid), F32),
            pltpu.VMEM((n_bins, width), F32),
            pltpu.VMEM((n_bins, hid), F32),
            pltpu.VMEM((n_bins, width), F32),
            pltpu.VMEM((n_bins, hid), F32),
            pltpu.VMEM((length + 4 * seg, hid), BF16),
            pltpu.VMEM((length + 2 * seg, hid), BF16),
            pltpu.VMEM((length, width), F32),
            pltpu.VMEM((2, width, 3 * hid), BF16),
            pltpu.VMEM((n_seq, n_bins + n_seq, width), F32),
            pltpu.VMEM((n_seq + 2, n_bins + n_seq, width), F32),
            pltpu.VMEM((n_seq, n_bins, width), BF16),
            pltpu.VMEM((width, 3 * hid), F32),
            pltpu.VMEM((hid, width), F32),
            pltpu.VMEM((n_dp, width, hid), WIRE),
            pltpu.VMEM((n_dp - 1, width, hid), WIRE),
            pltpu.VMEM((n_dp, rows, hid), WIRE),
            pltpu.VMEM((n_dp, rows, hid), WIRE),
            pltpu.VMEM((n_seq, 2, piece, hid), F32),
            pltpu.VMEM((n_seq - 1, 2, piece, hid), F32),
            pltpu.VMEM((n_seq, 2 * piece + 32, hid), WIRE),
            pltpu.VMEM((n_seq, 2 * piece + 32, hid), WIRE),
            pltpu.VMEM((n_dp, n_seq, 2 * piece, hid), WIRE),
            pltpu.VMEM((n_seq + 2, 8, seg + 128), F32),
            pltpu.SemaphoreType.DMA((copies,)),
            pltpu.SemaphoreType.DMA((copies,)),
        ],
        compiler_params=pltpu.CompilerParams(
            collective_id=0, has_side_effects=True, vmem_limit_bytes=KERNEL_VMEM
        ),
    )(
        bases,
        stem_table,
        first_conv_taps,
        first_projection_weight,
        second_conv_taps,
        second_projection_weight,
        bin_weight,
        cotangent,
    )
    shapes = (preds_shape, sal_shape, conv_shape, proj_shape, conv_shape, proj_shape, bin_shape)
    return pl.pallas_call(
        store_kernel,
        out_shape=shapes,
        in_specs=[hbm] * 4,
        out_specs=(hbm,) * 7,
        scratch_shapes=[
            room(preds_shape),
            room(sal_shape),
            room(bin_shape),
            room(made[3]),
            room(conv_shape),
            room(proj_shape),
            room(conv_shape),
            room(proj_shape),
            pltpu.SemaphoreType.DMA((4,)),
            pltpu.SemaphoreType.DMA((7,)),
        ],
        compiler_params=pltpu.CompilerParams(vmem_limit_bytes=KERNEL_VMEM),
    )(*made)


def fits_fused(mesh):
    n_seq, n_dp = mesh.shape["seq"], mesh.shape["dp"]
    return n_seq == 8 and n_dp == 4


def solution(mesh):
    placed = (P("dp", "seq"), P(), P(), P(), P(), P(), P("seq", None), P("dp", "seq", None))
    return jax.shard_map(
        per_device_fused if fits_fused(mesh) else per_device,
        mesh=mesh,
        in_specs=placed,
        out_specs=(P("dp", "seq", None), P("dp", None, "seq"), P(), P(), P(), P(), P("seq", None)),
        check_vma=False,
    )
```

```python
import functools

import jax
import jax.numpy as jnp
from jax import lax
from jax.experimental import pallas as pl
from jax.experimental.pallas import tpu as pltpu
from jax.sharding import PartitionSpec as P

STEM = 15
POOL = 128


def passed_along(value, axis, steps):
    count = lax.axis_size(axis)
    first, last = (max(0, -steps), min(count, count - steps))
    return lax.ppermute(value, axis, [(source, source + steps) for source in range(first, last)])


def with_halo(cells, sides, width):
    for axis, dim in sides:
        count = lax.axis_size(axis)
        ends = count - 1
        head = lax.slice_in_dim(cells, 0, width, axis=dim)
        tail = lax.slice_in_dim(cells, cells.shape[dim] - width, cells.shape[dim], axis=dim)
        cells = jnp.concatenate(
            [
                lax.ppermute(tail, axis, [(i, (i + 1) % count) for i in range(ends)]),
                cells,
                lax.ppermute(head, axis, [((i + 1) % count, i) for i in range(ends)]),
            ],
            axis=dim,
        )
    return cells


def gelu_exact(value):
    return 0.5 * value * (1.0 + jax.scipy.special.erf(value * 0.7071067811865476))


def gelu_slope(value):
    return (
        0.5 * (1.0 + jax.scipy.special.erf(value * 0.7071067811865476))
        + value * jnp.exp(-0.5 * value * value) * 0.3989422804014327
    )


def tap_shift(values, hops):
    return passed_along(values, "seq", hops)


def grad_shift(values, hops):
    return passed_along(values, "seq", hops)


def reduce_grads(conv_raw, proj_raw):
    return lax.psum((conv_raw, proj_raw), ("seq", "dp"))


def residual_block_apply(stream, conv_w, proj_w, hops):
    act = gelu_exact(stream.astype(jnp.float32)).astype(jnp.bfloat16)
    before = tap_shift(act, hops)
    after = tap_shift(act, -hops)
    tap_before = jnp.dot(before, conv_w[0], preferred_element_type=jnp.float32).astype(jnp.bfloat16)
    tap_after = jnp.dot(after, conv_w[2], preferred_element_type=jnp.float32).astype(jnp.bfloat16)
    pre = jnp.dot(act, conv_w[1], preferred_element_type=jnp.float32)
    pre = pre + tap_before.astype(jnp.float32) + tap_after.astype(jnp.float32)
    inner = gelu_exact(pre).astype(jnp.bfloat16)
    result = (
        stream.astype(jnp.float32) + jnp.dot(inner, proj_w, preferred_element_type=jnp.float32)
    ).astype(jnp.bfloat16)
    return (result, (stream, act, before, after, pre, inner))


def residual_block_reverse(incoming, saved, conv_w, proj_w, hops):
    stream, act, before, after, pre, inner = saved
    grad_in = incoming.astype(jnp.bfloat16)
    inner_grad = jnp.dot(grad_in, proj_w.T, preferred_element_type=jnp.float32)
    pre_grad = (inner_grad * gelu_slope(pre)).astype(jnp.bfloat16)
    later = grad_shift(pre_grad, -hops)
    earlier = grad_shift(pre_grad, hops)
    proj_raw = jnp.dot(inner.T, grad_in, preferred_element_type=jnp.float32)
    middle = jnp.dot(act.T, pre_grad, preferred_element_type=jnp.float32)
    conv_raw = jnp.stack(
        [
            jnp.dot(before.T, pre_grad, preferred_element_type=jnp.float32),
            middle,
            jnp.dot(after.T, pre_grad, preferred_element_type=jnp.float32),
        ]
    )
    act_grad = jnp.dot(pre_grad, conv_w[1].T, preferred_element_type=jnp.float32)
    act_grad = act_grad + jnp.dot(later, conv_w[0].T, preferred_element_type=jnp.float32)
    act_grad = act_grad + jnp.dot(earlier, conv_w[2].T, preferred_element_type=jnp.float32)
    outgoing = incoming + act_grad * gelu_slope(stream.astype(jnp.float32))
    conv_sum, proj_sum = reduce_grads(conv_raw, proj_raw)
    return (outgoing, conv_sum, proj_sum)


def per_device(
    bases,
    stem_table,
    first_conv_taps,
    first_projection_weight,
    second_conv_taps,
    second_projection_weight,
    bin_weight,
    cotangent,
):
    length = bases.shape[1]
    width = stem_table.shape[1]
    half = STEM // 2
    bins_dev = length // POOL
    scale = float(lax.axis_size("dp") * lax.axis_size("seq") * length) ** (-0.5)
    padded_ids = with_halo(bases[0] + 1, (("seq", 0),), half)
    taps = jnp.stack([padded_ids[k : k + length] for k in range(STEM)], axis=1)
    letters = jnp.arange(1, 5, dtype=jnp.int32)
    codes = (
        (taps[:, :, None] == letters[None, None, :]).astype(jnp.bfloat16).reshape(length, 4 * STEM)
    )
    stem_pre = jnp.dot(codes, stem_table, preferred_element_type=jnp.float32)
    residual_input_level = gelu_exact(stem_pre).astype(jnp.bfloat16)
    residual_after_first, first_block_stash = residual_block_apply(
        residual_input_level, first_conv_taps, first_projection_weight, 1
    )
    residual_after_second, second_block_stash = residual_block_apply(
        residual_after_first, second_conv_taps, second_projection_weight, 2
    )
    pooled = jnp.mean(
        residual_after_second.astype(jnp.float32).reshape(bins_dev, POOL, width), axis=1
    )
    pooled_act = gelu_exact(pooled).astype(jnp.bfloat16)
    cot_rows = cotangent[0]
    gathered = lax.all_gather(pooled_act, "seq", axis=0, tiled=True)
    preds = lax.dot_general(
        bin_weight, gathered, (((1,), (1,)), ((), ())), preferred_element_type=jnp.float32
    ).astype(jnp.bfloat16)
    bin_part = jnp.dot(cot_rows, gathered, preferred_element_type=jnp.float32)
    summed = lax.psum_scatter(
        lax.dot_general(
            cot_rows, bin_weight, (((0,), (0,)), ((), ())), preferred_element_type=jnp.float32
        ),
        "seq",
        scatter_dimension=0,
        tiled=True,
    )
    bin_total = lax.psum(bin_part, "dp")
    pooled_grad = summed * gelu_slope(pooled)
    gradient_after_second = jnp.repeat(pooled_grad / POOL, POOL, axis=0)
    gradient_after_first, conv_two_sum, proj_two_sum = residual_block_reverse(
        gradient_after_second, second_block_stash, second_conv_taps, second_projection_weight, 2
    )
    gradient_input_level, conv_one_sum, proj_one_sum = residual_block_reverse(
        gradient_after_first, first_block_stash, first_conv_taps, first_projection_weight, 1
    )
    stem_grad = (gradient_input_level * gelu_slope(stem_pre)).astype(jnp.bfloat16)
    code_grad = jnp.dot(stem_grad, stem_table.T, preferred_element_type=jnp.float32)
    padded_grad = with_halo(code_grad.astype(jnp.bfloat16), (("seq", 0),), half).astype(
        code_grad.dtype
    )
    total = jnp.zeros((length, 4), jnp.float32)
    for k in range(STEM):
        start = 2 * half - k
        total = total + padded_grad[start : start + length, 4 * k : 4 * k + 4]
    return (
        preds[None],
        total.T[None],
        conv_one_sum * scale,
        proj_one_sum * scale,
        conv_two_sum * scale,
        proj_two_sum * scale,
        bin_total * scale,
    )


NN = (((1,), (0,)), ((), ()))
NT = (((1,), (1,)), ((), ()))
TN = (((0,), (0,)), ((), ()))
F32 = jnp.float32
BF16 = jnp.bfloat16
WIRE = jnp.bfloat16


def mm(left, right, dims=NN):
    return lax.dot_general(left, right, dims, preferred_element_type=F32)


def gelu_pair(value):
    cdf = 0.5 + 0.5 * lax.erf(value * 0.7071067811865476)
    slope = cdf + value * (jnp.exp(-0.5 * value * value) * 0.3989422804014327)
    return value * cdf, slope


def tower_kernel(
    n_seq,
    n_dp,
    scale,
    bases_ref,
    stem_ref,
    conv1_ref,
    proj1_ref,
    conv2_ref,
    proj2_ref,
    binw_ref,
    cot_ref,
    preds_ref,
    sal_ref,
    conv1_out,
    proj1_out,
    conv2_out,
    proj2_out,
    bin_out,
    ids,
    stem_pad,
    slope_stem,
    stream0,
    act0,
    slope0,
    slope_pre1,
    inner1,
    stream1,
    act1,
    slope1,
    slope_pre2,
    pooled,
    inner_sum,
    bin_grad,
    bin_inner,
    pg2,
    pg1,
    grad1,
    wcat,
    part_out,
    part_in,
    pool_all,
    bin_all,
    conv_acc,
    proj_acc,
    rs_out,
    rs_in,
    rs2_out,
    rs2_in,
    ag,
    ag_all,
    sal_out,
    sal_in,
    send_sem,
    recv_sem,
):
    seq = lax.axis_index("seq")
    dp = lax.axis_index("dp")
    length = bases_ref.shape[1]
    width = stem_ref.shape[1]
    hid = proj1_ref.shape[0]
    seg = length // n_seq
    per_seg = seg // POOL
    n_bins = n_seq * per_seg
    half = STEM // 2

    barrier = pltpu.get_barrier_semaphore()
    for i in range(1, n_seq):
        pl.semaphore_signal(
            barrier,
            inc=1,
            device_id=(lax.rem(seq + i, n_seq), dp),
            device_id_type=pl.DeviceIdType.MESH,
        )
    for i in range(1, n_dp):
        pl.semaphore_signal(
            barrier,
            inc=1,
            device_id=(seq, lax.rem(dp + i, n_dp)),
            device_id_type=pl.DeviceIdType.MESH,
        )
    used = [0]

    def send(axis, source, target):
        count = n_seq if axis == "seq" else n_dp
        copies = []
        for i in range(1, count):
            if axis == "seq":
                peer = lax.rem(seq + i, count)
                where = (peer, dp)
            else:
                peer = lax.rem(dp + i, count)
                where = (seq, peer)
            slot = used[0]
            used[0] += 1
            copy = pltpu.make_async_remote_copy(
                src_ref=source(peer),
                dst_ref=target(i),
                send_sem=send_sem.at[slot],
                recv_sem=recv_sem.at[slot],
                device_id=where,
                device_id_type=pl.DeviceIdType.MESH,
            )
            copy.start()
            copies.append(copy)
        return copies

    def finish(copies):
        for copy in copies:
            copy.wait()

    def rows_of(chunk):
        return pl.ds(pl.multiple_of(chunk * seg, seg), seg)

    outside = jnp.full((1, 1, length), -1, jnp.int32)
    ids[pl.ds(0, 1)] = outside
    ids[pl.ds(n_seq + 1, 1)] = outside
    ids[pl.ds(seq + 1, 1)] = bases_ref[...].reshape(1, 1, length)
    pl.semaphore_wait(barrier, n_seq - 1 + n_dp - 1)
    ids_copies = send("seq", lambda peer: ids.at[seq + 1], lambda i: ids.at[seq + 1])

    bins_total = n_bins * n_seq
    nat = lax.broadcasted_iota(jnp.int32, (bins_total, bins_total), 0)
    got = lax.broadcasted_iota(jnp.int32, (bins_total, bins_total), 1)
    h_bits = per_seg.bit_length() - 1
    s_bits = n_seq.bit_length() - 1
    chunk_of = nat >> (h_bits + s_bits)
    owner_of = (nat >> h_bits) & (n_seq - 1)
    place = (owner_of << (h_bits + s_bits)) | (chunk_of << h_bits) | (nat & (per_seg - 1))
    perm = (place == got).astype(F32).astype(BF16)

    cot = cot_ref[...].reshape(cot_ref.shape[1], cot_ref.shape[2])
    cot_perm = mm(cot, perm).astype(BF16)
    part_out[...] = mm(cot_perm, binw_ref[...], TN).reshape(n_seq, n_bins, width)
    part_copies = send("seq", lambda peer: part_out.at[peer], lambda i: part_in.at[i - 1])

    stem_pad[...] = jnp.concatenate(
        [stem_ref[...].astype(F32), jnp.zeros((64 - 4 * STEM, width), F32)], axis=0
    ).astype(BF16)
    wcat[0] = jnp.concatenate([conv1_ref[0], conv1_ref[1], conv1_ref[2]], axis=1)
    wcat[1] = jnp.concatenate([conv2_ref[0], conv2_ref[1], conv2_ref[2]], axis=1)
    act0[pl.ds(0, seg)] = jnp.zeros((seg, width), BF16)
    act0[pl.ds((n_seq + 1) * seg, seg)] = jnp.zeros((seg, width), BF16)
    act1[pl.ds(0, 2 * seg)] = jnp.zeros((2 * seg, width), BF16)
    act1[pl.ds((n_seq + 2) * seg, 2 * seg)] = jnp.zeros((2 * seg, width), BF16)
    pg1[pl.ds(0, seg)] = jnp.zeros((seg, hid), BF16)
    pg1[pl.ds((n_seq + 1) * seg, seg)] = jnp.zeros((seg, hid), BF16)
    pg2[pl.ds(0, 2 * seg)] = jnp.zeros((2 * seg, hid), BF16)
    pg2[pl.ds((n_seq + 2) * seg, 2 * seg)] = jnp.zeros((2 * seg, hid), BF16)
    sal_out[...] = jnp.zeros_like(sal_out)
    pooled[...] = jnp.zeros_like(pooled)
    inner_sum[...] = jnp.zeros_like(inner_sum)

    first = (seq == 0).astype(jnp.int32)
    last = (seq == n_seq - 1).astype(jnp.int32)
    low = pl.multiple_of(lax.rem(seq * seg + length - 128, length), 128)
    high = pl.multiple_of(lax.rem(seq * seg + seg, length), 128)
    span = seg + 256
    finish(ids_copies)

    def stem_chunk(chunk, carry):
        line = jnp.concatenate(
            [
                ids[chunk + 1 - first, :, pl.ds(low, 128)],
                ids[chunk + 1, :, pl.ds(pl.multiple_of(seq * seg, seg), seg)],
                ids[chunk + 1 + last, :, pl.ds(high, 128)],
            ],
            axis=1,
        )
        block = jnp.broadcast_to(line, (8, span))
        sub = lax.broadcasted_iota(jnp.int32, (8, span), 0)
        block = jnp.where(sub < 4, block, pltpu.roll(block, span - 1, 1))
        letter = (sub & 3)[:, :seg]
        tiles = []
        for m in range(8):
            moved = pltpu.roll(block, span - (128 - half + 2 * m), 1)[:, :seg]
            tiles.append((moved == letter).astype(F32))
        codes = jnp.concatenate(tiles, axis=0).astype(BF16)
        pre = mm(codes, stem_pad[...], TN)
        value, slope = gelu_pair(pre)
        rows = rows_of(chunk)
        slope_stem[rows] = slope
        value = value.astype(BF16)
        stream0[rows] = value
        act, slope = gelu_pair(value.astype(F32))
        slope0[rows] = slope
        act0[rows_of(chunk + 1)] = act.astype(BF16)
        return carry

    lax.fori_loop(0, n_seq, stem_chunk, 0)

    def pre_of(act, conv_ref, chunk, hops):
        wide = jnp.concatenate(
            [act[rows_of(chunk)], act[rows_of(chunk + hops)], act[rows_of(chunk + 2 * hops)]],
            axis=1,
        )
        return mm(wide, conv_ref[...].reshape(3 * width, hid))

    def first_chunk(chunk, carry):
        rows = rows_of(chunk)
        inner, slope = gelu_pair(pre_of(act0, conv1_ref, chunk, 1))
        slope_pre1[rows] = slope
        inner = inner.astype(BF16)
        inner1[rows] = inner
        result = (stream0[rows].astype(F32) + mm(inner, proj1_ref[...])).astype(BF16)
        stream1[rows] = result
        act, slope = gelu_pair(result.astype(F32))
        slope1[rows] = slope
        act1[rows_of(chunk + 2)] = act.astype(BF16)
        return carry

    lax.fori_loop(0, n_seq, first_chunk, 0)

    def second_chunk(chunk, carry):
        rows = rows_of(chunk)
        inner, slope = gelu_pair(pre_of(act1, conv2_ref, chunk, 2))
        slope_pre2[rows] = slope
        inner = inner.astype(BF16)
        result = (stream1[rows].astype(F32) + mm(inner, proj2_ref[...])).astype(BF16)
        bin_row = lax.broadcasted_iota(jnp.int32, (n_bins, seg), 0)
        bin_pos = lax.broadcasted_iota(jnp.int32, (n_bins, seg), 1) // POOL
        member = (bin_row == bin_pos + chunk * per_seg).astype(F32).astype(BF16)
        pooled[...] += mm(member, result)
        inner_sum[...] += mm(member, inner)
        return carry

    lax.fori_loop(0, n_seq, second_chunk, 0)

    pooled_act, pooled_slope = gelu_pair(pooled[...] * (1.0 / POOL))
    pool_all[pl.ds(seq, 1)] = pooled_act.astype(BF16).reshape(1, n_bins, width)
    pool_copies = send("seq", lambda peer: pool_all.at[seq], lambda i: pool_all.at[seq])

    finish(part_copies)
    total = part_out[seq]
    for i in range(n_seq - 1):
        total = total + part_in[i]
    grad2 = total * pooled_slope * (1.0 / POOL)
    bin_grad[...] = grad2
    grad2_in = grad2.astype(BF16)
    bin_inner[...] = mm(grad2_in, proj2_ref[...], NT)

    isum = inner_sum[...]
    coarse = isum.astype(BF16)
    fine = (isum - coarse.astype(F32)).astype(BF16)
    proj_acc[...] = mm(coarse, grad2_in, TN) + mm(fine, grad2_in, TN)

    def spread(ref, chunk, columns):
        return jnp.concatenate(
            [
                jnp.broadcast_to(ref[pl.ds(chunk * per_seg + h, 1), :], (POOL, columns))
                for h in range(per_seg)
            ],
            axis=0,
        )

    def grad2_chunk(chunk, carry):
        wide = spread(bin_inner, chunk, hid)
        pg2[rows_of(chunk + 2)] = (wide * slope_pre2[rows_of(chunk)]).astype(BF16)
        return carry

    lax.fori_loop(0, n_seq, grad2_chunk, 0)

    def around(pg, chunk, hops):
        return jnp.concatenate(
            [pg[rows_of(chunk + 2 * hops)], pg[rows_of(chunk + hops)], pg[rows_of(chunk)]], axis=1
        )

    def conv_grads(act, pg, hops):
        conv_acc[...] = jnp.zeros_like(conv_acc)

        def step(chunk, carry):
            conv_acc[...] += mm(act[rows_of(chunk + hops)], around(pg, chunk, hops), TN)
            return carry

        lax.fori_loop(0, n_seq, step, 0)

    piece = width // n_seq

    def reduce_one(b):
        for t in range(3):
            rs_out[b, t] = conv_acc[:, t * hid : (t + 1) * hid].astype(WIRE)
        for t in range(width // hid):
            rs_out[b, 3, pl.ds(t * hid, hid)] = proj_acc[:, t * hid : (t + 1) * hid].astype(WIRE)
        return send("dp", lambda peer: rs_out.at[b, peer], lambda i: rs_in.at[b, i - 1])

    def reduce_two(b, copies):
        finish(copies)
        total = rs_out[b, dp].astype(F32)
        for i in range(n_dp - 1):
            total = total + rs_in[b, i].astype(F32)
        rs2_out[b] = total.reshape(n_seq, piece, hid)
        return send("seq", lambda peer: rs2_out.at[b, peer], lambda i: rs2_in.at[b, i - 1])

    def reduce_three(b, copies):
        finish(copies)
        total = rs2_out[b, seq]
        for i in range(n_seq - 1):
            total = total + rs2_in[b, i]
        ag[b, pl.ds(seq, 1)] = (total * scale).astype(WIRE).reshape(1, piece, hid)
        return send("seq", lambda peer: ag.at[b, seq], lambda i: ag.at[b, seq])

    def reduce_four(b, copies):
        finish(copies)
        ag_all[b, pl.ds(dp, 1)] = ag[b].reshape(1, n_seq, piece, hid)
        return send("dp", lambda peer: ag.at[b], lambda i: ag_all.at[b, dp])

    def reduce_end(b, copies, conv_out, proj_out):
        finish(copies)
        for t in range(3):
            conv_out[t] = ag_all[b, t].reshape(width, hid).astype(F32)
        whole = ag_all[b, 3].reshape(width, hid).astype(F32)
        for t in range(width // hid):
            proj_out[:, t * hid : (t + 1) * hid] = whole[t * hid : (t + 1) * hid]

    conv_grads(act1, pg2, 2)
    two = reduce_one(0)

    finish(pool_copies)
    natural = mm(perm, pool_all[...].reshape(bins_total, width)).astype(BF16)
    preds_ref[...] = mm(binw_ref[...], natural, NT).astype(BF16).reshape(preds_ref.shape)
    bin_all[pl.ds(dp, 1)] = (
        mm(cot, natural).astype(WIRE).reshape(1, binw_ref.shape[0], width)
    )
    bin_copies = send("dp", lambda peer: bin_all.at[dp], lambda i: bin_all.at[dp])

    proj_acc[...] = jnp.zeros_like(proj_acc)

    def grad1_chunk(chunk, carry):
        rows = rows_of(chunk)
        act_grad = mm(around(pg2, chunk, 2), wcat[1], NT)
        grad = spread(bin_grad, chunk, width) + act_grad * slope1[rows]
        grad1[rows] = grad
        grad_in = grad.astype(BF16)
        pg1[rows_of(chunk + 1)] = (mm(grad_in, proj1_ref[...], NT) * slope_pre1[rows]).astype(BF16)
        proj_acc[...] += mm(inner1[rows], grad_in, TN)
        return carry

    lax.fori_loop(0, n_seq, grad1_chunk, 0)
    two = reduce_two(0, two)
    conv_grads(act0, pg1, 1)
    one = reduce_one(1)
    two = reduce_three(0, two)

    wide_out = seg + 128

    def saliency_chunk(chunk, carry):
        rows = rows_of(chunk)
        act_grad = mm(around(pg1, chunk, 1), wcat[0], NT)
        grad = grad1[rows] + act_grad * slope0[rows]
        stem_grad = (grad * slope_stem[rows]).astype(BF16)
        code_grad = mm(stem_pad[...], stem_grad, NT)
        code_grad = jnp.concatenate([code_grad, jnp.zeros((64, 128), F32)], axis=1)
        total = jnp.zeros((8, wide_out), F32)
        for m in range(8):
            shift = (2 * m - half) % wide_out
            tile = code_grad[8 * m : 8 * m + 8]
            total = total + (pltpu.roll(tile, shift, 1) if shift else tile)
        total = total[:4] + pltpu.roll(total, 1, 1)[4:]
        sal_out[chunk + 1, pl.ds(0, 4)] = total
        sal_out[chunk + 1 + jnp.where(seq == 0, -1, 1), pl.ds(4, 4)] = total
        return carry

    middle = n_seq // 2
    lax.fori_loop(0, middle, saliency_chunk, 0)
    one = reduce_two(1, one)
    two = reduce_four(0, two)
    lax.fori_loop(middle, n_seq, saliency_chunk, 0)
    sal_in[pl.ds(seq, 1)] = sal_out[pl.ds(seq + 1, 1)]
    sal_copies = send("seq", lambda peer: sal_out.at[peer + 1], lambda i: sal_in.at[seq])
    one = reduce_three(1, one)

    finish(bin_copies)
    total = bin_all[0].astype(F32)
    for d in range(1, n_dp):
        total = total + bin_all[d].astype(F32)
    bin_out[...] = total * scale
    reduce_end(0, two, conv2_out, proj2_out)
    one = reduce_four(1, one)

    finish(sal_copies)
    lane = lax.broadcasted_iota(jnp.int32, (4, 128), 1)

    def rest(s, row):
        return sal_in[s, row : row + 4, seg:]

    for s in range(n_seq):
        before = rest(s - 1, 0) if s > 0 else rest(n_seq - 1, 4)
        after = rest(s + 1, 0) if s < n_seq - 1 else rest(0, 4)
        block = sal_in[s, 0:4, 0:seg]
        sal_ref[0, :, s * seg : s * seg + 128] = block[:, :128] + jnp.where(lane < 64, before, 0.0)
        if seg > 256:
            sal_ref[0, :, s * seg + 128 : (s + 1) * seg - 128] = block[:, 128 : seg - 128]
        sal_ref[0, :, (s + 1) * seg - 128 : (s + 1) * seg] = block[:, seg - 128 :] + jnp.where(
            lane >= 64, after, 0.0
        )
    reduce_end(1, one, conv1_out, proj1_out)


def store_kernel(*refs):
    sems = refs[-1]
    count = (len(refs) - 1) // 2
    copies = [
        pltpu.make_async_copy(refs[i], refs[count + i], sems.at[i]) for i in range(count)
    ]
    for copy in copies:
        copy.start()
    for copy in copies:
        copy.wait()


def per_device_fused(
    bases,
    stem_table,
    first_conv_taps,
    first_projection_weight,
    second_conv_taps,
    second_projection_weight,
    bin_weight,
    cotangent,
):
    n_seq, n_dp = lax.axis_size("seq"), lax.axis_size("dp")
    length = bases.shape[1]
    width = stem_table.shape[1]
    hid = first_projection_weight.shape[0]
    seg = length // n_seq
    n_bins = length // POOL
    chans = bin_weight.shape[0]
    scale = float(n_dp * n_seq * length) ** (-0.5)
    copies = 5 * (n_seq - 1) + (n_dp - 1) + 2 * (2 * (n_seq - 1) + 2 * (n_dp - 1))
    vmem = pl.BlockSpec(memory_space=pltpu.VMEM)
    sds = jax.ShapeDtypeStruct
    piece = width // n_seq
    made = pl.pallas_call(
        functools.partial(tower_kernel, n_seq, n_dp, scale),
        out_shape=(
            sds((1, chans, cotangent.shape[2]), BF16),
            sds((1, 4, length), F32),
            sds((3, width, hid), F32),
            sds((hid, width), F32),
            sds((3, width, hid), F32),
            sds((hid, width), F32),
            sds((chans, width), F32),
        ),
        in_specs=[vmem] * 8,
        out_specs=(vmem,) * 7,
        scratch_shapes=[
            pltpu.VMEM((n_seq + 2, 1, length), jnp.int32),
            pltpu.VMEM((64, width), BF16),
            pltpu.VMEM((length, width), F32),
            pltpu.VMEM((length, width), BF16),
            pltpu.VMEM((length + 2 * seg, width), BF16),
            pltpu.VMEM((length, width), F32),
            pltpu.VMEM((length, hid), F32),
            pltpu.VMEM((length, hid), BF16),
            pltpu.VMEM((length, width), BF16),
            pltpu.VMEM((length + 4 * seg, width), BF16),
            pltpu.VMEM((length, width), F32),
            pltpu.VMEM((length, hid), F32),
            pltpu.VMEM((n_bins, width), F32),
            pltpu.VMEM((n_bins, hid), F32),
            pltpu.VMEM((n_bins, width), F32),
            pltpu.VMEM((n_bins, hid), F32),
            pltpu.VMEM((length + 4 * seg, hid), BF16),
            pltpu.VMEM((length + 2 * seg, hid), BF16),
            pltpu.VMEM((length, width), F32),
            pltpu.VMEM((2, width, 3 * hid), BF16),
            pltpu.VMEM((n_seq, n_bins, width), F32),
            pltpu.VMEM((n_seq - 1, n_bins, width), F32),
            pltpu.VMEM((n_seq, n_bins, width), BF16),
            pltpu.VMEM((n_dp, chans, width), WIRE),
            pltpu.VMEM((width, 3 * hid), F32),
            pltpu.VMEM((hid, width), F32),
            pltpu.VMEM((2, n_dp, width, hid), WIRE),
            pltpu.VMEM((2, n_dp - 1, width, hid), WIRE),
            pltpu.VMEM((2, n_seq, piece, hid), F32),
            pltpu.VMEM((2, n_seq - 1, piece, hid), F32),
            pltpu.VMEM((2, n_seq, piece, hid), WIRE),
            pltpu.VMEM((2, n_dp, n_seq, piece, hid), WIRE),
            pltpu.VMEM((n_seq + 2, 8, seg + 128), F32),
            pltpu.VMEM((n_seq, 8, seg + 128), F32),
            pltpu.SemaphoreType.DMA((copies,)),
            pltpu.SemaphoreType.DMA((copies,)),
        ],
        compiler_params=pltpu.CompilerParams(
            collective_id=0, has_side_effects=True, vmem_limit_bytes=48 * 1024 * 1024
        ),
    )(
        bases,
        stem_table,
        first_conv_taps,
        first_projection_weight,
        second_conv_taps,
        second_projection_weight,
        bin_weight,
        cotangent,
    )
    return pl.pallas_call(
        store_kernel,
        out_shape=tuple(sds(leaf.shape, leaf.dtype) for leaf in made),
        in_specs=[vmem] * len(made),
        out_specs=(pl.BlockSpec(memory_space=pl.ANY),) * len(made),
        scratch_shapes=[pltpu.SemaphoreType.DMA((len(made),))],
        compiler_params=pltpu.CompilerParams(vmem_limit_bytes=2 * 1024 * 1024),
    )(*made)


def fits_fused(mesh):
    n_seq, n_dp = mesh.shape["seq"], mesh.shape["dp"]
    return n_seq in (2, 4, 8) and n_dp == 4


def solution(mesh):
    placed = (P("dp", "seq"), P(), P(), P(), P(), P(), P("seq", None), P("dp", "seq", None))
    return jax.shard_map(
        per_device_fused if fits_fused(mesh) else per_device,
        mesh=mesh,
        in_specs=placed,
        out_specs=(P("dp", "seq", None), P("dp", None, "seq"), P(), P(), P(), P(), P("seq", None)),
        check_vma=False,
    )
```
